32 devices in a mesh: wave: 8 (over y, x, core), lev: 4 (over z).
Axes of the slice: x: 2, y: 2, z: 4, core: 2. Of those that a mesh axis runs over, the one named last changes fastest.
Arguments:
- spectral: bfloat16 [320, 2, 16, 641], P('wave', None, 'lev'), may hold values from -6 to 6
- legendre: bfloat16 [320, 641, 640], P('wave'), as said below
- quad_weights: float32 [640], replicated, as said below
- pair_order: int32 [320], replicated, may hold values from 0 to 319, as said below
- lon_counts: int32 [1280], replicated, may hold values from 20 to 2560
- vertical: bfloat16 [16, 16], replicated, may hold values from -1.5 to 1.5
- wind_field: bfloat16 [1280, 16, 2560], P('wave', 'lev'), may hold values from -6 to 6
Outputs:
- spectral_tendency: float32 [320, 2, 16, 641], P('wave', None, 'lev')
The draws below stay inside these ranges and needn't reach their ends.
Inputs may be any that keep to these rules, and one draw needn't show every extreme that they name: Each pair index appears once; slot s holds the wavenumbers pair_order[s] and 639 - pair_order[s], and the rows of spectral and legendre in slot s follow it. legendre[s, r, j] is the associated Legendre function of row r's degree and wavenumber, normalized so that the integral of its square over mu = cos(colatitude) from -1 to 1 is 1, at the node j of quad_weights; the southern node 1279 - j mirrors node j. `quad_weights`: Positive.
All inputs are finite; a program needn't handle non-finite values.
Results may differ from the reference program's by a relative error of at most 0.0077.
Values may be sent and summed in bfloat16 or wider, within the bound.
No kernel may reach another device: no remote copies, remote signals or barrier semaphores. Data moves between devices by JAX's collectives and lax.ppermute only.
A program may use at most 128 MiB of HBM per device.

```python
import math
import jax
import jax.numpy as jnp
from jax import lax

M = 640
NLAT = 1280
NLON = 2560
LEVELS = 16
PAIRS = 320
ROWS = 641
NHALF = 640
N_WAVE = 8


def latitude_nodes(key):
    jitter_key = jax.random.fold_in(key, 11)
    weight_key = jax.random.fold_in(key, 12)
    jitter = jax.random.uniform(jitter_key, (NHALF,), jnp.float32, -0.25, 0.25)
    spread = jax.random.uniform(weight_key, (NHALF,), jnp.float32, 0.7, 1.3)
    colatitude = math.pi * (jnp.arange(NHALF, dtype=jnp.float32) + 0.5 + jitter) / NLAT
    sine_values = jnp.sin(colatitude)
    return (jnp.cos(colatitude), sine_values, math.pi / NLAT * sine_values * spread)


def pair_permutation(key):
    return jax.random.permutation(jax.random.fold_in(key, 21), PAIRS).astype(jnp.int32)


def draw_pair_order(key, part):
    return pair_permutation(key)


def draw_quad_weights(key, part):
    return latitude_nodes(key)[2].astype(jnp.float32)


def draw_lon_counts(key, part):
    lat_index = jnp.arange(NLAT, dtype=jnp.int32)
    distance = jnp.minimum(lat_index, NLAT - 1 - lat_index)
    jitter_steps = jax.random.randint(jax.random.fold_in(key, 31), (NLAT,), 0, 4)
    return jnp.minimum(NLON, 20 + 4 * distance + 4 * jitter_steps).astype(jnp.int32)


def draw_legendre(key, part):
    cosines, sine_values, _ = latitude_nodes(key)
    permuted = pair_permutation(key)
    orders = jnp.arange(1, M, dtype=jnp.float32)
    log_steps = 0.5 * jnp.log((2.0 * orders + 1.0) / (2.0 * orders))
    diag_log = jnp.concatenate([jnp.zeros((1,), jnp.float32), jnp.cumsum(log_steps)]) + 0.5 * math.log(0.5)
    log_sines = jnp.log(sine_values)

    def one_pair(low_wave):
        pair_waves = jnp.stack([low_wave, M - 1 - low_wave])
        degrees = pair_waves.astype(jnp.float32)
        diagonal_start = jnp.exp(diag_log[pair_waves][:, None] + degrees[:, None] * log_sines[None, :])

        def advance(recurrence, degree):
            prev_one, prev_two = recurrence
            degree_value = degree.astype(jnp.float32)
            alpha_coef = jnp.sqrt((4.0 * degree_value ** 2 - 1.0) / jnp.maximum(degree_value ** 2 - degrees ** 2, 1.0))
            beta_coef = jnp.sqrt(jnp.maximum((degree_value - 1.0) ** 2 - degrees ** 2, 0.0) / jnp.maximum(4.0 * (degree_value - 1.0) ** 2 - 1.0, 1.0))
            recurred = alpha_coef[:, None] * (cosines[None, :] * prev_one - beta_coef[:, None] * prev_two)
            above = (degree_value > degrees)[:, None]
            equal = (degree_value == degrees)[:, None]
            current = jnp.where(equal, diagonal_start, jnp.where(above, recurred, 0.0))
            return ((current, prev_one), current)
        zeros_start = jnp.zeros((2, NHALF), jnp.float32)
        _, values = lax.scan(advance, (zeros_start, zeros_start), jnp.arange(M, dtype=jnp.int32))
        row_ids = jnp.arange(M + 1, dtype=jnp.int32)
        in_first = row_ids < M - low_wave
        degree_index = jnp.where(in_first, low_wave + row_ids, row_ids - 1)
        which_wave = jnp.where(in_first, 0, 1)
        return values[degree_index, which_wave]
    packed = lax.map(one_pair, permuted)
    return packed.astype(jnp.bfloat16)


def levels(stream_key, extent, split, low, largest):
    factor_of = 1.0
    for position, shards_of in split:
        heights = jax.random.uniform(jax.random.fold_in(jax.random.fold_in(stream_key, 6), position), (shards_of,), jnp.float32, low / len(split), largest / len(split))
        factor_of = factor_of * jnp.repeat(jnp.exp(heights), extent[position] // shards_of).reshape((-1,) + (1,) * (len(extent) - 1 - position))
    return factor_of


def noise(key, extent, scale, bound, split=(), kind=jnp.bfloat16):
    level = levels(key, extent, split, -0.22, 0.18) if split else 1.0
    result = jax.random.normal(key, extent, jnp.float32) * scale * level
    return jnp.minimum(jnp.maximum(result, -bound), bound).astype(kind)


def setup_inputs(seed: int = 0) -> dict:
    streams_of = jax.random.split(jax.random.key(seed), 8)
    spectral = noise(streams_of[0], (PAIRS, 2, LEVELS, ROWS), 1.0, 6.0, ((0, 8), (2, 4)))
    legendre = draw_legendre(jax.random.fold_in(streams_of[7], 71), 0)
    quad_weights = draw_quad_weights(jax.random.fold_in(streams_of[7], 71), 0)
    pair_order = draw_pair_order(jax.random.fold_in(streams_of[7], 71), 0)
    lon_counts = draw_lon_counts(jax.random.fold_in(streams_of[7], 71), 0)
    vertical = noise(streams_of[5], (LEVELS, LEVELS), LEVELS ** -0.5, 1.5)
    wind_field = noise(streams_of[6], (NLAT, LEVELS, NLON), 1.0, 6.0, ((0, 8), (1, 4)))
    return {"spectral": spectral, "legendre": legendre, "quad_weights": quad_weights, "pair_order": pair_order, "lon_counts": lon_counts, "vertical": vertical, "wind_field": wind_field}


def row_layout(low_waves, row_count, total_waves):
    row_ids = jnp.arange(row_count, dtype=jnp.int32)[None, :]
    in_first = row_ids < (total_waves - low_waves[:, None])
    degree_gap = jnp.where(in_first, row_ids, row_ids - total_waves + low_waves[:, None])
    return in_first.astype(jnp.float32), (degree_gap % 2).astype(jnp.float32)


def fourier_basis(wavenumbers, lon_count):
    longitudes = jnp.arange(lon_count, dtype=jnp.int32)
    phases = (wavenumbers[:, None] * longitudes[None, :]) % lon_count
    angles = phases.astype(jnp.float32) * (2.0 * math.pi / lon_count)
    factor = jnp.where(wavenumbers == 0, 1.0, 2.0).astype(jnp.float32)
    basis = jnp.stack([factor[:, None] * jnp.cos(angles), -factor[:, None] * jnp.sin(angles)], axis=1)
    return basis.astype(jnp.bfloat16), factor


def reference(spectral, legendre, quad_weights, pair_order, lon_counts, vertical, wind_field):
    first_part, parity = row_layout(pair_order, M + 1, M)
    slot_pick = jnp.stack([first_part, 1.0 - first_part], axis=1)
    parity_pick = jnp.stack([1.0 - parity, parity], axis=1)
    vertical_wide = vertical.astype(jnp.float32)
    mixed = jnp.einsum("kl,pclr->pckr", vertical_wide, spectral.astype(jnp.float32)).astype(jnp.bfloat16)

    def inverse_pair(inputs):
        coefs, table_rows, slots, parities = inputs
        selector = slots[:, None, :] * parities[None, :, :]
        masked = selector[:, :, None, None, :] * coefs.astype(jnp.float32)[None, None]
        partial_value = jnp.einsum("tqrlx,xj->tqrlj", masked, table_rows.astype(jnp.float32))
        symmetric = partial_value[:, 0]
        antisymmetric = partial_value[:, 1]
        joined = jnp.concatenate([symmetric + antisymmetric, (symmetric - antisymmetric)[..., ::-1]], axis=-1)
        return joined.astype(jnp.bfloat16)

    fourier = lax.map(inverse_pair, (mixed, legendre, slot_pick, parity_pick)).reshape(M, 2, LEVELS, NLAT)
    wavenumbers = jnp.stack([pair_order, M - 1 - pair_order], axis=1).reshape(M)
    basis, factor = fourier_basis(wavenumbers, NLON)
    basis_wide = basis.astype(jnp.float32)
    band_lats = NLAT // N_WAVE
    blocks = jnp.moveaxis(fourier.reshape(M, 2, LEVELS, N_WAVE, band_lats), 3, 0)
    wind_blocks = wind_field.reshape(N_WAVE, band_lats, LEVELS, NLON)
    count_blocks = lon_counts.reshape(N_WAVE, band_lats)

    def grid_band(inputs):
        coefs, winds, counts = inputs
        retained = (2 * wavenumbers[:, None] < counts[None, :]).astype(jnp.float32)
        masked = coefs.astype(jnp.float32) * retained[:, None, None, :]
        grid_values = jnp.einsum("mrlj,mrn->jln", masked, basis_wide).astype(jnp.bfloat16)
        grid_values = lax.optimization_barrier(grid_values)
        forcing = (winds.astype(jnp.float32) * grid_values.astype(jnp.float32)).astype(jnp.bfloat16)
        transformed = jnp.einsum("jln,mrn->mrlj", forcing.astype(jnp.float32), basis_wide)
        rescale = retained / (factor[:, None] * NLON)
        return (transformed * rescale[:, None, None, :]).astype(jnp.bfloat16)

    returned = lax.map(grid_band, (blocks, wind_blocks, count_blocks))
    fourier_back = jnp.moveaxis(returned, 0, 3).reshape(PAIRS, 2, 2, LEVELS, NLAT)

    def forward_pair(inputs):
        coefs, table_rows, slots, parities = inputs
        northern = coefs[..., :NHALF].astype(jnp.float32)
        southern = coefs[..., NHALF:][..., ::-1].astype(jnp.float32)
        even_part = ((northern + southern) * quad_weights).astype(jnp.bfloat16)
        odd_part = ((northern - southern) * quad_weights).astype(jnp.bfloat16)
        folded = jnp.stack([even_part, odd_part], axis=1).astype(jnp.float32)
        products = jnp.einsum("xj,tqrlj->tqrlx", table_rows.astype(jnp.float32), folded)
        selector = slots[:, None, :] * parities[None, :, :]
        return jnp.sum(products * selector[:, :, None, None, :], axis=(0, 1))

    return lax.map(forward_pair, (fourier_back, legendre, slot_pick, parity_pick))
```

```python
import functools
import math

import jax
import jax.numpy as jnp
from jax import lax
from jax.experimental import pallas as pl
from jax.experimental.pallas import tpu as pltpu
from jax.sharding import PartitionSpec as P


GROUP = 8
RBLOCK = 128
F32 = jnp.float32
BF16 = jnp.bfloat16


def params(**kw):
    return pltpu.CompilerParams(vmem_limit_bytes=56 * 1024 * 1024, **kw)


def class_masks(low_ref, first_row, count, total):
    shape = (GROUP, count * GROUP)
    lane = lax.broadcasted_iota(jnp.int32, shape, 1)
    sub = lax.broadcasted_iota(jnp.int32, shape, 0)
    own = (lane & (GROUP - 1)) == sub
    r = (lane >> 3) + first_row
    start = total - low_ref[:, :1]
    first = r < start
    gap = jnp.where(first, r, r - start)
    code = jnp.where(first, 0, 1) + 2 * (gap & 1)
    return [own & (code == k) for k in range(4)]


def tail_parity(low_ref, r, total, width):
    gap = r - total + low_ref[:, :1]
    return jnp.broadcast_to((gap & 1) == 1, (GROUP, width))


def inverse_kernel(me_ref, vert_ref, low_ref, rep_ref, flip_ref, leg_ref, *rest, shapes, n_src, extra):
    CL, L, C, R, J, W, band = shapes
    srcs = rest[:n_src]
    rest = rest[n_src:]
    add_ref = None
    if extra:
        add_ref, rest = rest[0], rest[1:]
    out_ref, mix_ref, lhs_ref = rest
    total = R - 1
    full = R // RBLOCK
    for c in range(C):
        sums = [None] * L
        k = 0
        for src in srcs:
            for s in range(src.shape[0]):
                for li in range(L):
                    x = src[s, c * L + li].astype(F32)
                    for lo in range(L):
                        term = vert_ref[k, lo, li] * x
                        sums[lo] = term if sums[lo] is None else sums[lo] + term
                k += 1
        for lo in range(L):
            v = sums[lo]
            if extra:
                v = v + add_ref[0, c * L + lo].astype(F32)
            mix_ref[c * L + lo] = v.astype(BF16).astype(F32)
    for b in range(full):
        masks = class_masks(low_ref, b * RBLOCK, RBLOCK, total)
        a = mix_ref[:, :, b * RBLOCK : (b + 1) * RBLOCK].reshape(CL * GROUP, RBLOCK)
        spread = jnp.dot(a.astype(BF16), rep_ref[...], preferred_element_type=F32)
        for cl in range(CL):
            x = spread[cl * GROUP : (cl + 1) * GROUP]
            for q in range(2):
                rows = jnp.concatenate(
                    [jnp.where(masks[2 * q + t], x, 0.0) for t in range(2)], axis=0
                )
                lo = cl * 32 + q * 16
                lhs_ref[lo : lo + 16, b * RBLOCK * GROUP : (b + 1) * RBLOCK * GROUP] = rows.astype(BF16)
    table = leg_ref.reshape(R * GROUP, J)
    acc = jnp.dot(
        lhs_ref[...], table[0 : full * RBLOCK * GROUP, :], preferred_element_type=F32
    )
    acc = acc.reshape(CL, 4, GROUP, J)
    sym = [[acc[cl, t] for t in range(2)] for cl in range(CL)]
    anti = [[acc[cl, 2 + t] for t in range(2)] for cl in range(CL)]
    for r in range(full * RBLOCK, R):
        row = leg_ref[r].astype(F32)
        odd = tail_parity(low_ref, r, total, J)
        for cl in range(CL):
            term = mix_ref[cl, :, r : r + 1] * row
            sym[cl][1] = sym[cl][1] + jnp.where(odd, 0.0, term)
            anti[cl][1] = anti[cl][1] + jnp.where(odd, term, 0.0)
    sym = [jnp.concatenate(v, axis=0) for v in sym]
    anti = [jnp.concatenate(v, axis=0) for v in anti]
    north = [sym[cl] + anti[cl] for cl in range(CL)]
    south = jnp.concatenate([sym[cl] - anti[cl] for cl in range(CL)], axis=0).astype(BF16)
    south = jnp.dot(south, flip_ref[...], preferred_element_type=F32)
    half = W // 2
    for w in range(W):
        slot = me_ref[0] ^ w if W <= 8 else w
        lo = (w % half) * band
        for c in range(C):
            pieces = []
            for l in range(L):
                cl = c * L + l
                v = north[cl] if w < half else south[cl * 16 : (cl + 1) * 16]
                pieces.append(v[:, lo : lo + band])
            out_ref[slot, 0, c * 16 : (c + 1) * 16, :] = jnp.concatenate(pieces, axis=1).astype(BF16)


def mix_kernel(vert_ref, *rest, L, C):
    srcs, out_ref = rest[:-1], rest[-1]
    for c in range(C):
        sums = [None] * L
        for k, src in enumerate(srcs):
            for li in range(L):
                x = src[0, c * L + li].astype(F32)
                for lo in range(L):
                    term = vert_ref[k, lo, li] * x
                    sums[lo] = term if sums[lo] is None else sums[lo] + term
        for lo in range(L):
            out_ref[0, c * L + lo] = sums[lo].astype(BF16)


def basis_kernel(cos_ref, sin_ref, dcos_ref, dsin_ref, out_ref, *, steps):
    c, s = cos_ref[...], sin_ref[...]
    dc, ds = dcos_ref[...], dsin_ref[...]
    for a in range(steps):
        out_ref[:, 0:16, a * 128 : (a + 1) * 128] = c.astype(BF16)
        out_ref[:, 16:32, a * 128 : (a + 1) * 128] = (-s).astype(BF16)
        c, s = c * dc - s * ds, s * dc + c * ds


def grid_kernel(counts_ref, *rest, n_parts, n_chunks):
    parts = rest[:n_parts]
    bases = rest[n_parts : n_parts + n_chunks]
    m2_ref, wind_ref, out_ref, flat_ref, turned_ref = rest[n_parts + n_chunks :]
    rows = flat_ref.shape[0]

    @pl.when(pl.program_id(0) == 0)
    def _():
        at = 0
        for part in parts:
            n = part.shape[0] * part.shape[1]
            flat_ref[at : at + n, :] = part[...].reshape(n, part.shape[2])
            at += n
        for lo in range(0, rows, 128):
            hi = min(lo + 128, rows)
            keep = m2_ref[lo:hi, :1] < counts_ref[...]
            v = jnp.where(keep, flat_ref[lo:hi, :].astype(F32), 0.0)
            turned_ref[:, lo:hi] = v.T.astype(BF16)

    acc, at = None, 0
    for basis in bases:
        n = basis.shape[0]
        v = jnp.dot(turned_ref[:, at : at + n], basis[...], preferred_element_type=F32)
        acc = v if acc is None else acc + v
        at += n
    values = acc.astype(BF16).astype(F32)
    out_ref[...] = (wind_ref[...].astype(F32) * values).astype(BF16)


def back_kernel(counts_ref, basis_ref, m2_ref, scale_ref, forcing_ref, out_ref):
    v = lax.dot_general(
        basis_ref[...], forcing_ref[...], (((1,), (1,)), ((), ())), preferred_element_type=F32
    )
    keep = m2_ref[:, :1] < counts_ref[...]
    v = jnp.where(keep, v * scale_ref[:, :1], 0.0)
    out_ref[...] = v.reshape(out_ref.shape).astype(BF16)


def forward_kernel(me_ref, low_ref, rep_ref, flip_ref, quad_ref, leg_ref, *rest, shapes, n_parts):
    CL, L, C, R, J, W, band = shapes
    parts = rest[:n_parts]
    out_ref, bands_ref, fold_ref = rest[n_parts:]
    total = R - 1
    full = R // RBLOCK
    half = W // 2
    k = 0
    for part in parts:
        for s in range(part.shape[0]):
            slot = me_ref[0] ^ k if W <= 8 else k
            bands_ref[slot] = part[s, 0].astype(F32)
            k += 1
    quad = quad_ref[...]
    for l in range(L):
        cut = slice(l * band, (l + 1) * band)
        north = jnp.concatenate([bands_ref[w, :, cut] for w in range(half)], axis=1)
        south = jnp.concatenate([bands_ref[w, :, cut] for w in range(half, W)], axis=1)
        south = jnp.dot(south.astype(BF16), flip_ref[...], preferred_element_type=F32)
        even = (north + south) * quad
        odd = (north - south) * quad
        for c in range(C):
            lo = (c * L + l) * 32
            fold_ref[lo : lo + 16, :] = even[c * 16 : (c + 1) * 16].astype(BF16)
            fold_ref[lo + 16 : lo + 32, :] = odd[c * 16 : (c + 1) * 16].astype(BF16)
    table = leg_ref.reshape(R * GROUP, J)
    width = RBLOCK * GROUP
    for b in range(full):
        masks = class_masks(low_ref, b * RBLOCK, RBLOCK, total)
        res = lax.dot_general(
            fold_ref[...],
            table[b * width : (b + 1) * width, :],
            (((1,), (1,)), ((), ())),
            preferred_element_type=F32,
        )
        kept = []
        for cl in range(CL):
            v = jnp.zeros((GROUP, width), F32)
            for k in range(4):
                lo = cl * 32 + k * GROUP
                v = jnp.where(masks[k], res[lo : lo + GROUP], v)
            kept.append(v)
        kept = jnp.concatenate(kept, axis=0)
        high = kept.astype(BF16)
        low = (kept - high.astype(F32)).astype(BF16)
        dims = (((1,), (1,)), ((), ()))
        packed = lax.dot_general(high, rep_ref[...], dims, preferred_element_type=F32)
        packed = packed + lax.dot_general(low, rep_ref[...], dims, preferred_element_type=F32)
        out_ref[:, :, b * RBLOCK : (b + 1) * RBLOCK] = packed.reshape(CL, GROUP, RBLOCK)
    for r in range(full * RBLOCK, R):
        row = leg_ref[r].astype(F32)
        odd = tail_parity(low_ref, r, total, J)
        for cl in range(CL):
            even_rows = fold_ref[cl * 32 : cl * 32 + 16, :].astype(F32)[GROUP:]
            odd_rows = fold_ref[cl * 32 + 16 : cl * 32 + 32, :].astype(F32)[GROUP:]
            v = jnp.where(odd, odd_rows, even_rows) * row
            out_ref[cl, :, r : r + 1] = jnp.sum(v, axis=1, keepdims=True)


def whole(shape):
    return pl.BlockSpec(shape, lambda *_: (0,) * len(shape))


SMEM = pl.BlockSpec(memory_space=pltpu.SMEM)


def exchange(sent, count):
    if count > 8:
        return [lax.all_to_all(sent, "wave", 0, 0, tiled=True)]
    parts = [sent[0:1]]
    for d in range(1, count):
        parts.append(lax.ppermute(sent[d : d + 1], "wave", [(i, i ^ d) for i in range(count)]))
    return parts


def shards(spectral, legendre, quad_weights, pair_order, lon_counts, vertical, wind_field):
    W, Z = lax.axis_size("wave"), lax.axis_size("lev")
    pairs, C, L, R = spectral.shape
    J = legendre.shape[2]
    band, NX = wind_field.shape[0], wind_field.shape[2]
    CL, LJ, total = C * L, L * band, R - 1
    me, z = lax.axis_index("wave"), lax.axis_index("lev")
    padded = -(-pairs // GROUP) * GROUP
    NG = padded // GROUP
    chunks = [(0, NG)]
    pads = padded - pairs

    own = spectral.transpose(1, 2, 0, 3).reshape(CL, pairs, R)
    own = jnp.pad(own, ((0, 0), (0, pads), (0, 0)))
    table = jnp.pad(legendre.transpose(1, 0, 2), ((0, 0), (0, pads), (0, 0)))

    own_pairs = pair_order.reshape(W, pairs)
    all_pairs = jnp.pad(own_pairs, ((0, 0), (0, pads)))
    lows = lax.dynamic_index_in_dim(all_pairs, me, 0, keepdims=False)
    lows = jnp.broadcast_to(lows[:, None], (padded, 128))
    if W <= 8:
        all_pairs = all_pairs[me ^ jnp.arange(W)]
    all_pairs = all_pairs.reshape(W, NG, 1, GROUP)
    waves = jnp.concatenate([all_pairs, total - 1 - all_pairs], axis=2).reshape(W, NG, 16)

    rep = (
        jnp.arange(RBLOCK)[:, None] == jnp.arange(RBLOCK * GROUP)[None, :] // GROUP
    ).astype(BF16)
    flip = (jnp.arange(J)[:, None] + jnp.arange(J)[None, :] == J - 1).astype(BF16)
    counts = lax.dynamic_slice_in_dim(lon_counts, me * band, band)
    counts = jnp.tile(counts, L)[None, :]
    wind = wind_field.transpose(1, 0, 2).reshape(LJ, NX)
    me_arr = me.astype(jnp.int32).reshape(1)
    quad = quad_weights[None, :]
    shapes = (CL, L, C, R, J, W, band)

    vert = vertical.astype(F32).reshape(Z, L, Z, L)

    def vblock(rows, cols):
        v = lax.dynamic_index_in_dim(vert, rows, 0, keepdims=False)
        return lax.dynamic_index_in_dim(v, cols, 1, keepdims=False)

    waves_flat = waves[:, :, :, None]
    lane = jnp.arange(128, dtype=jnp.int32)
    unit = 2.0 * math.pi / NX
    factor = jnp.where(waves_flat == 0, 1.0, 2.0).astype(F32)
    start_angle = (waves_flat * lane % NX).astype(F32) * unit
    step_angle = (waves_flat * 128 % NX).astype(F32) * unit
    cos0, sin0 = factor * jnp.cos(start_angle), factor * jnp.sin(start_angle)
    dcos = jnp.broadcast_to(jnp.cos(step_angle), cos0.shape)
    dsin = jnp.broadcast_to(jnp.sin(step_angle), cos0.shape)

    def lows_of(g0, G):
        return lows[g0 * GROUP : (g0 + G) * GROUP]

    leg_spec = lambda g0: pl.BlockSpec((R, GROUP, J), lambda g: (0, g + g0, 0))
    low_spec = lambda g0: pl.BlockSpec((GROUP, 128), lambda g: (g + g0, 0))

    gathered = []
    for g0, G in chunks:
        x = own[:, g0 * GROUP : (g0 + G) * GROUP][None]
        if Z == 4:
            pair = [(0, 1), (1, 0), (2, 3), (3, 2)]
            middle = [(1, 2), (2, 1)]
            ends = [(1, 0), (2, 3)]
            a = lax.ppermute(x, "lev", pair)
            b = lax.ppermute(x, "lev", middle)
            c = lax.ppermute(a, "lev", middle)
            table_d = jnp.stack([vblock(z ^ 1, 3 - z), vblock(z ^ 1, (3 - z) ^ 1)])
            spec = pl.BlockSpec((1, CL, GROUP, R), lambda g: (0, 0, g, 0))
            part = pl.pallas_call(
                functools.partial(mix_kernel, L=L, C=C),
                grid=(G,),
                out_shape=jax.ShapeDtypeStruct(x.shape, BF16),
                in_specs=[SMEM, spec, spec],
                out_specs=spec,
                compiler_params=params(),
                name="partial_levels",
            )(table_d, b, c)
            d = lax.ppermute(part, "lev", ends)
            tab = jnp.stack(
                [vblock(z, z), vblock(z, z ^ 1), vblock(z, 3 - z), vblock(z, (3 - z) ^ 1)]
            )
            gathered.append(((x, a, b, c), d, tab))
        else:
            every = lax.all_gather(x, "lev", axis=0, tiled=True)
            tab = lax.dynamic_index_in_dim(vert, z, 0, keepdims=False).transpose(1, 0, 2)
            gathered.append(((every,), None, tab))

    bases, m2s, scales = [], [], []
    for g0, G in chunks:
        cut = lambda v: v[:, g0 : g0 + G].reshape((W * G, 16, 128))
        per = G
        block = pl.BlockSpec((per, 16, 128), lambda i: (i, 0, 0))
        basis = pl.pallas_call(
            functools.partial(basis_kernel, steps=NX // 128),
            grid=(W * G // per,),
            out_shape=jax.ShapeDtypeStruct((W * G, 32, NX), BF16),
            in_specs=[block] * 4,
            out_specs=pl.BlockSpec((per, 32, NX), lambda i: (i, 0, 0)),
            compiler_params=params(),
            cost_estimate=pl.CostEstimate(
                flops=W * G * 16 * NX * 8, bytes_accessed=W * G * 32 * NX * 2, transcendentals=0
            ),
            name="basis",
        )(cut(cos0), cut(sin0), cut(dcos), cut(dsin))
        bases.append(basis.reshape(W * G * 32, NX))
        m = waves[:, g0 : g0 + G, None, :]
        m = jnp.broadcast_to(m, (W, G, 2, 16)).reshape(W * G * 32, 1)
        m2s.append(jnp.broadcast_to(2 * m, (W * G * 32, 128)))
        f = jnp.where(m == 0, 1.0, 2.0).astype(F32)
        scales.append(jnp.broadcast_to(1.0 / (f * NX), (W * G * 32, 128)))

    arrived = []
    for (g0, G), (srcs, extra, tab) in zip(chunks, gathered):
        specs = [
            pl.BlockSpec((s.shape[0], CL, GROUP, R), lambda g: (0, 0, g, 0)) for s in srcs
        ]
        args = list(srcs)
        if extra is not None:
            specs.append(pl.BlockSpec((1, CL, GROUP, R), lambda g: (0, 0, g, 0)))
            args.append(extra)
        sent = pl.pallas_call(
            functools.partial(
                inverse_kernel, shapes=shapes, n_src=len(srcs), extra=extra is not None
            ),
            grid=(G,),
            out_shape=jax.ShapeDtypeStruct((W, G, 32, LJ), BF16),
            in_specs=[SMEM, SMEM, low_spec(g0), whole(rep.shape), whole(flip.shape), leg_spec(g0)]
            + specs,
            out_specs=pl.BlockSpec((W, 1, 32, LJ), lambda g: (0, g, 0, 0)),
            scratch_shapes=[
                pltpu.VMEM((CL, GROUP, R), F32),
                pltpu.VMEM((CL * 32, R // RBLOCK * RBLOCK * GROUP), BF16),
            ],
            compiler_params=params(),
            cost_estimate=pl.CostEstimate(
                flops=2 * G * CL * 32 * R * GROUP * J,
                bytes_accessed=G * R * GROUP * J * 2,
                transcendentals=0,
            ),
            name="inverse_legendre",
        )(me_arr, tab, lows, rep, flip, table, *args)
        arrived.append(exchange(sent, W))

    parts = [p.reshape(-1, 32, LJ) for chunk in arrived for p in chunk]
    rows = W * padded * 4
    XB = 512
    forcing = pl.pallas_call(
        functools.partial(grid_kernel, n_parts=len(parts), n_chunks=len(bases)),
        grid=(NX // XB,),
        out_shape=jax.ShapeDtypeStruct((LJ, NX), BF16),
        in_specs=[whole(counts.shape)]
        + [whole(p.shape) for p in parts]
        + [pl.BlockSpec((b.shape[0], XB), lambda i: (0, i)) for b in bases]
        + [whole((rows, 128)), pl.BlockSpec((LJ, XB), lambda i: (0, i))],
        out_specs=pl.BlockSpec((LJ, XB), lambda i: (0, i)),
        scratch_shapes=[pltpu.VMEM((rows, LJ), BF16), pltpu.VMEM((LJ, rows), BF16)],
        compiler_params=params(),
        cost_estimate=pl.CostEstimate(
            flops=2 * rows * LJ * NX, bytes_accessed=2 * NX * (rows + 2 * LJ), transcendentals=0
        ),
        name="grid_points",
    )(counts, *parts, *bases, jnp.concatenate(m2s, axis=0), wind)

    results = []
    for (g0, G), basis, m2, scale in zip(chunks, bases, m2s, scales):
        n = basis.shape[0]
        steps = 2
        per = n // steps
        sent = pl.pallas_call(
            back_kernel,
            grid=(steps,),
            out_shape=jax.ShapeDtypeStruct((n // 32, 32, LJ), BF16),
            in_specs=[
                whole(counts.shape),
                pl.BlockSpec((per, NX), lambda i: (i, 0)),
                pl.BlockSpec((per, 128), lambda i: (i, 0)),
                pl.BlockSpec((per, 128), lambda i: (i, 0)),
                whole((LJ, NX)),
            ],
            out_specs=pl.BlockSpec((per // 32, 32, LJ), lambda i: (i, 0, 0)),
            compiler_params=params(),
            cost_estimate=pl.CostEstimate(
                flops=2 * n * LJ * NX, bytes_accessed=2 * NX * (n + LJ), transcendentals=0
            ),
            name="back_transform",
        )(counts, basis, m2, scale, forcing)
        returned = exchange(sent.reshape(W, G, 32, LJ), W)
        out = pl.pallas_call(
            functools.partial(forward_kernel, shapes=shapes, n_parts=len(returned)),
            grid=(G,),
            out_shape=jax.ShapeDtypeStruct((CL, G * GROUP, R), F32),
            in_specs=[
                SMEM, low_spec(g0), whole(rep.shape), whole(flip.shape), whole(quad.shape),
                leg_spec(g0),
            ]
            + [pl.BlockSpec((p.shape[0], 1, 32, LJ), lambda g: (0, g, 0, 0)) for p in returned],
            out_specs=pl.BlockSpec((CL, GROUP, R), lambda g: (0, g, 0)),
            scratch_shapes=[
                pltpu.VMEM((W, 32, LJ), F32),
                pltpu.VMEM((CL * 32, J), BF16),
            ],
            compiler_params=params(),
            cost_estimate=pl.CostEstimate(
                flops=2 * G * CL * 32 * R * GROUP * J,
                bytes_accessed=G * R * GROUP * J * 2,
                transcendentals=0,
            ),
            name="forward_legendre",
        )(me_arr, lows, rep, flip, quad, table, *returned)
        results.append(out)
    out = jnp.concatenate(results, axis=1)[:, :pairs]
    return out.reshape(C, L, pairs, R).transpose(2, 0, 1, 3)


def solution(mesh):
    return jax.shard_map(
        shards,
        mesh=mesh,
        in_specs=(
            P("wave", None, "lev", None),
            P("wave", None, None),
            P(),
            P(),
            P(),
            P(),
            P("wave", "lev", None),
        ),
        out_specs=P("wave", None, "lev", None),
        check_vma=False,
    )
```

```python
import functools
import math

import jax
import jax.numpy as jnp
import numpy as np
from jax import lax
from jax.experimental import pallas as pl
from jax.experimental.pallas import tpu as pltpu
from jax.sharding import PartitionSpec as P


GROUP = 8
RBLOCK = 128
F32 = jnp.float32
BF16 = jnp.bfloat16


LEVEL_PIECES = (2, 3)
BACK_PIECES = (3, 2)


def XOR_ORDER(count):
    return count <= 8


def pieces(sizes, count):
    out, at = [], 0
    for size in sizes if sum(sizes) == count else (count,):
        out.append((at, size))
        at += size
    return out


def params(**kw):
    return pltpu.CompilerParams(vmem_limit_bytes=56 * 1024 * 1024, **kw)


def class_masks(low_ref, first_row, count, total):
    shape = (GROUP, count // 2 * GROUP)
    lane = lax.broadcasted_iota(jnp.int32, shape, 1)
    sub = lax.broadcasted_iota(jnp.int32, shape, 0)
    own = (lane & (GROUP - 1)) == sub
    low = low_ref[:, :1]
    masks = []
    for parity in range(2):
        first = (lane >> 3) * 2 + (first_row + parity) < total - low
        wave = jnp.where(first, low, total - 1 - low)
        masks.append([own & ((wave & 1) == s) for s in range(2)])
    return masks


def flipped(low_ref, width):
    return jnp.broadcast_to((low_ref[:, :1] & 1) == 1, (GROUP, width))


def tail_masks(low_ref, total, width):
    wave = jnp.broadcast_to(total - 1 - low_ref[:, :1], (GROUP, width))
    return [(wave & 1) == s for s in range(2)]


def mirror(x, flip):
    n, width = x.shape
    tiles = width // 128
    v = jnp.concatenate([x[:, k * 128 : (k + 1) * 128] for k in range(tiles)], axis=0)
    v = jnp.dot(v, flip, preferred_element_type=F32)
    return jnp.concatenate([v[k * n : (k + 1) * n] for k in reversed(range(tiles))], axis=1)


def inverse_kernel(me_ref, vert_ref, low_ref, rep_ref, flip_ref, leg_ref, *rest, shapes, n_src, extra):
    CL, L, C, R, J, W, band = shapes
    srcs = rest[:n_src]
    rest = rest[n_src:]
    add_ref = None
    if extra:
        add_ref, rest = rest[0], rest[1:]
    bands_ref, mix_ref, lhs_ref = rest[-3:]
    out_refs = rest[-3 - (W if XOR_ORDER(W) else 1) : -3]
    total = R - 1
    full = R // RBLOCK
    for c in range(C):
        sums = [None] * L
        k = 0
        for src in srcs:
            for s in range(src.shape[0]):
                for li in range(L):
                    x = src[s, c * L + li].astype(F32)
                    for lo in range(L):
                        term = vert_ref[k, lo, li] * x
                        sums[lo] = term if sums[lo] is None else sums[lo] + term
                k += 1
        for lo in range(L):
            v = sums[lo]
            if extra:
                v = v + add_ref[0, c * L + lo].astype(F32)
            mix_ref[c * L + lo] = v.astype(BF16).astype(F32)
    blocks = [
        mix_ref[:, :, b * RBLOCK : (b + 1) * RBLOCK].reshape(CL * GROUP, RBLOCK)
        for b in range(full)
    ]
    spread = jnp.dot(
        jnp.concatenate(blocks, axis=0).astype(BF16), rep_ref[...], preferred_element_type=F32
    )
    width = RBLOCK * GROUP // 2
    for b in range(full):
        masks = class_masks(low_ref, b * RBLOCK, RBLOCK, total)
        for cl in range(CL):
            at = (b * CL + cl) * GROUP
            for parity in range(2):
                x = spread[at : at + GROUP, parity * width : (parity + 1) * width]
                rows = jnp.concatenate(
                    [jnp.where(masks[parity][s], x, 0.0) for s in range(2)], axis=0
                )
                lhs_ref[parity, cl * 16 : (cl + 1) * 16, b * width : (b + 1) * width] = rows.astype(
                    BF16
                )
    table = leg_ref.at[0 : full * RBLOCK].reshape(full * RBLOCK // 2, 2 * GROUP, J)
    kept = []
    for parity in range(2):
        rows = table[:, parity * GROUP : (parity + 1) * GROUP].reshape(full * width, J)
        acc = jnp.dot(lhs_ref[parity], rows, preferred_element_type=F32).reshape(CL, 2, GROUP, J)
        kept.append([[acc[cl, s] for s in range(2)] for cl in range(CL)])
    for r in range(full * RBLOCK, R):
        row = leg_ref[r].astype(F32)
        masks = tail_masks(low_ref, total, J)
        for cl in range(CL):
            term = mix_ref[cl, :, r : r + 1] * row
            for s in range(2):
                kept[r % 2][cl][s] = kept[r % 2][cl][s] + jnp.where(masks[s], term, 0.0)
    flips = flipped(low_ref, J)
    north, south = [], []
    for cl in range(CL):
        even, odd = kept[0][cl], kept[1][cl]
        north.append([even[s] + odd[s] for s in range(2)])
        less = [even[s] - odd[s] for s in range(2)]
        south += [jnp.where(flips, -less[0], less[0]), less[1]]
    south = mirror(jnp.concatenate(south, axis=0).astype(BF16), flip_ref[...])
    half = W // 2
    for w in range(W):
        lo = (w % half) * band
        for s in range(2):
            both = []
            for c in range(C):
                pieces = []
                for l in range(L):
                    cl = c * L + l
                    at = cl * 16 + s * GROUP
                    v = north[cl][s] if w < half else south[at : at + GROUP]
                    pieces.append(v[:, lo : lo + band])
                both.append(jnp.concatenate(pieces, axis=1))
            bands_ref[w, s * 16 : (s + 1) * 16, :] = jnp.concatenate(both, axis=0).astype(BF16)
    if XOR_ORDER(W):
        for d in range(W):
            out_refs[d][0] = bands_ref[me_ref[0] ^ d]
    else:
        out_refs[0][:, 0] = bands_ref[...]


def mix_kernel(vert_ref, *rest, L, C):
    srcs, out_ref = rest[:-1], rest[-1]
    for c in range(C):
        sums = [None] * L
        for k, src in enumerate(srcs):
            for li in range(L):
                x = src[0, c * L + li].astype(F32)
                for lo in range(L):
                    term = vert_ref[k, lo, li] * x
                    sums[lo] = term if sums[lo] is None else sums[lo] + term
        for lo in range(L):
            out_ref[0, c * L + lo] = sums[lo].astype(BF16)


def turn(phase, period):
    x = phase.astype(F32) * (4.0 / period)
    quarter = jnp.floor(x + 0.5)
    y = phase.astype(F32) - quarter * (period / 4)
    y = y * (2.0 * math.pi / period)
    z = y * y
    s = y * (1.0 + z * (-1.0 / 6 + z * (1.0 / 120 + z * (-1.0 / 5040 + z * (1.0 / 362880)))))
    c = 1.0 + z * (-0.5 + z * (1.0 / 24 + z * (-1.0 / 720 + z * (1.0 / 40320))))
    k = quarter.astype(jnp.int32)
    swap = (k & 1) == 1
    cos = jnp.where(swap, s, c)
    sin = jnp.where(swap, c, s)
    cos = jnp.where(((k + 1) & 2) == 2, -cos, cos)
    sin = jnp.where((k & 2) == 2, -sin, sin)
    return cos, sin


def basis_kernel(wave_ref, even_ref, odd_ref, *, steps, NX):
    lane = lax.broadcasted_iota(jnp.int32, (1, 1, 128), 2)
    for k, ref in enumerate((even_ref, odd_ref)):
        m = wave_ref[k].reshape(-1, 2, GROUP, 128)[:, 0]
        c, s = turn(m * lane, NX)
        dc, ds = turn(m * 128, NX)
        factor = jnp.where(m == 0, 1.0, 2.0)
        c, s = c * factor, s * factor
        for a in range(steps):
            v = jnp.concatenate([c, -s], axis=1).astype(BF16)
            ref[:, a * 128 : (a + 1) * 128] = v.reshape(-1, 128)
            c, s = c * dc - s * ds, s * dc + c * ds


def grid_kernel(counts_ref, *rest, n_parts, W, chunks, NX):
    parts = rest[:n_parts]
    even_ref, odd_ref, wave_ref, near_ref, far_ref = rest[n_parts : n_parts + 5]
    out_refs = rest[n_parts + 5 : -3]
    flat_ref, turned_ref, back_ref = rest[-3:]
    rows = flat_ref.shape[1]
    LJ = counts_ref.shape[1]
    step = pl.program_id(0)

    @pl.when(step == 0)
    def _():
        at = 0
        for part in parts:
            many = len(part.shape) == 4
            for i in range(part.shape[0] if many else 1):
                for g in range(part.shape[-3]):
                    to = (g * W + at) * 16
                    v = part[i, g] if many else part[g]
                    for s in range(2):
                        flat_ref[s, to : to + 16, :] = v[s * 16 : (s + 1) * 16]
                at += 1
        for s in range(2):
            for lo in range(0, rows, 128):
                hi = min(lo + 128, rows)
                keep = 2 * wave_ref[s, lo:hi, :1] < counts_ref[...]
                v = jnp.where(keep, flat_ref[s, lo:hi, :].astype(F32), 0.0).astype(BF16)
                turned_ref[s, :, lo:hi] = v.T
        back_ref[...] = jnp.zeros_like(back_ref)

    bases = (even_ref, odd_ref)
    even = jnp.dot(turned_ref[0], even_ref[...], preferred_element_type=F32)
    odd = jnp.dot(turned_ref[1], odd_ref[...], preferred_element_type=F32)
    near = near_ref[...] * (even + odd).astype(BF16)
    far = far_ref[...] * (even - odd).astype(BF16)
    for s, forcing in enumerate((near + far, near - far)):
        back_ref[s] += lax.dot_general(
            bases[s][...], forcing, (((1,), (1,)), ((), ())), preferred_element_type=F32
        )

    @pl.when(step == pl.num_programs(0) - 1)
    def _():
        for s in range(2):
            m = wave_ref[s][:, :1]
            scale = jnp.where(m == 0, 1.0 / NX, 0.5 / NX)
            v = jnp.where(2 * m < counts_ref[...], back_ref[s] * scale, 0.0).astype(BF16)
            k = 0
            for g0, G in chunks:
                for d in range(W):
                    for g in range(G):
                        at = ((g0 + g) * W + d) * 16
                        if XOR_ORDER(W):
                            out_refs[k + d][g, s * 16 : (s + 1) * 16, :] = v[at : at + 16]
                        else:
                            out_refs[k][d, g, s * 16 : (s + 1) * 16, :] = v[at : at + 16]
                k += W if XOR_ORDER(W) else 1


def forward_kernel(me_ref, low_ref, rep_ref, flip_ref, quad_ref, leg_ref, *rest, shapes, n_parts):
    CL, L, C, R, J, W, band = shapes
    parts = rest[:n_parts]
    out_ref, bands_ref, fold_ref, kept_ref = rest[-4:]
    total = R - 1
    full = R // RBLOCK
    half = W // 2
    k = 0
    for part in parts:
        many = len(part.shape) == 4
        for i in range(part.shape[0] if many else 1):
            slot = me_ref[0] ^ k if XOR_ORDER(W) else k
            bands_ref[slot] = (part[i, 0] if many else part[0]).astype(F32)
            k += 1
    quad = quad_ref[...]
    norths, souths = [], []
    for l in range(L):
        cut = slice(l * band, (l + 1) * band)
        norths.append(jnp.concatenate([bands_ref[w, :, cut] for w in range(half)], axis=1))
        souths.append(jnp.concatenate([bands_ref[w, :, cut] for w in range(half, W)], axis=1))
    souths = mirror(jnp.concatenate(souths, axis=0).astype(BF16), flip_ref[...])
    flips = flipped(low_ref, J)
    for l in range(L):
        south = souths[l * 32 : (l + 1) * 32]
        even = (norths[l] + south) * quad
        odd = (norths[l] - south) * quad
        for c in range(C):
            at = (c * L + l) * 16
            for parity, (v, u) in enumerate(((even, odd), (odd, even))):
                lo, hi = c * GROUP, 16 + c * GROUP
                first = jnp.where(flips, u[lo : lo + GROUP], v[lo : lo + GROUP])
                rows = jnp.concatenate([first, v[hi : hi + GROUP]], axis=0)
                fold_ref[parity, at : at + 16, :] = rows.astype(BF16)
    width = RBLOCK * GROUP // 2
    n = CL * GROUP
    table = leg_ref.at[0 : full * RBLOCK].reshape(full * RBLOCK // 2, 2 * GROUP, J)
    for parity in range(2):
        rows = table[:, parity * GROUP : (parity + 1) * GROUP].reshape(full * width, J)
        res = lax.dot_general(
            fold_ref[parity], rows, (((1,), (1,)), ((), ())), preferred_element_type=F32
        )
        for b in range(full):
            masks = class_masks(low_ref, b * RBLOCK, RBLOCK, total)[parity]
            for cl in range(0, CL, 2):
                pair = []
                for i in range(cl, cl + 2):
                    own = [
                        res[i * 16 + s * GROUP : i * 16 + (s + 1) * GROUP, b * width : (b + 1) * width]
                        for s in range(2)
                    ]
                    v = jnp.where(masks[0], own[0], jnp.where(masks[1], own[1], 0.0))
                    pair.append(v)
                v = jnp.concatenate(pair, axis=0)
                high = v.astype(BF16)
                at = b * n + cl * GROUP
                cut = slice(parity * width, (parity + 1) * width)
                kept_ref[at : at + 16, cut] = high
                kept_ref[full * n + at : full * n + at + 16, cut] = (v - high.astype(F32)).astype(BF16)
    packed = lax.dot_general(
        kept_ref[...], rep_ref[...], (((1,), (1,)), ((), ())), preferred_element_type=F32
    )
    packed = packed[: full * n] + packed[full * n :]
    for b in range(full):
        v = jnp.swapaxes(packed[b * n : (b + 1) * n].reshape(CL, GROUP, RBLOCK), 0, 1)
        for c in range(C):
            out_ref[:, c, :, b * RBLOCK : (b + 1) * RBLOCK] = v[:, c * L : (c + 1) * L]
    for r in range(full * RBLOCK, R):
        row = leg_ref[r].astype(F32)
        masks = tail_masks(low_ref, total, J)
        for cl in range(CL):
            rows = fold_ref[r % 2, cl * 16 : (cl + 1) * 16, :].astype(F32)
            v = jnp.where(masks[0], rows[:GROUP], jnp.where(masks[1], rows[GROUP:], 0.0))
            v = jnp.sum(v * row, axis=1, keepdims=True)
            out_ref[:, cl // L, cl % L, r : r + 1] = v


def whole(shape):
    return pl.BlockSpec(shape, lambda *_: (0,) * len(shape))


SMEM = pl.BlockSpec(memory_space=pltpu.SMEM)


def exchange(sent, count):
    if not XOR_ORDER(count):
        return [lax.all_to_all(sent[0], "wave", 0, 0, tiled=True)]
    parts = [sent[0]]
    for d in range(1, count):
        parts.append(lax.ppermute(sent[d], "wave", [(i, i ^ d) for i in range(count)]))
    return parts


def travel_shapes(W, groups, width):
    if XOR_ORDER(W):
        return [jax.ShapeDtypeStruct((groups, 32, width), BF16)] * W
    return [jax.ShapeDtypeStruct((W, groups, 32, width), BF16)]


def group_spec(shape, first):
    if len(shape) == 3:
        return pl.BlockSpec((1,) + shape[1:], lambda g: (g + first, 0, 0))
    return pl.BlockSpec((shape[0], 1) + shape[2:], lambda g: (0, g + first, 0, 0))


def shards(spectral, legendre, quad_weights, pair_order, lon_counts, vertical, wind_field):
    W, Z = lax.axis_size("wave"), lax.axis_size("lev")
    pairs, C, L, R = spectral.shape
    J = legendre.shape[2]
    band, NX = wind_field.shape[0], wind_field.shape[2]
    CL, LJ, total = C * L, L * band, R - 1
    me, z = lax.axis_index("wave"), lax.axis_index("lev")
    padded = -(-pairs // GROUP) * GROUP
    NG = padded // GROUP
    chunks = pieces(LEVEL_PIECES, NG)
    pads = padded - pairs

    own = spectral.transpose(1, 2, 0, 3).reshape(CL, pairs, R)
    own = jnp.pad(own, ((0, 0), (0, pads), (0, 0)))
    table = jnp.pad(legendre.transpose(1, 0, 2), ((0, 0), (0, pads), (0, 0)))

    own_pairs = pair_order.reshape(W, pairs)
    all_pairs = jnp.pad(own_pairs, ((0, 0), (0, pads)))
    lows = lax.dynamic_index_in_dim(all_pairs, me, 0, keepdims=False)
    lows = jnp.broadcast_to(lows[:, None], (padded, 128))
    if XOR_ORDER(W):
        all_pairs = all_pairs[me ^ jnp.arange(W)]
    all_pairs = all_pairs.reshape(W, NG, 1, GROUP)
    others = total - 1 - all_pairs
    is_odd = (all_pairs & 1) == 1
    evens = jnp.where(is_odd, others, all_pairs)
    waves = jnp.stack([evens, total - 1 - evens]).transpose(0, 2, 1, 3, 4)
    rows = NG * W * 16
    waves = jnp.broadcast_to(waves, (2, NG, W, 2, GROUP)).reshape(2, rows, 1)
    waves = jnp.broadcast_to(waves, (2, rows, 128))

    lane = np.arange(RBLOCK * GROUP)[None, :]
    half_width = RBLOCK * GROUP // 2
    rep = np.arange(RBLOCK)[:, None] == lane % half_width // GROUP * 2 + lane // half_width
    rep = jnp.asarray(rep, BF16)
    flip = jnp.asarray(np.arange(128)[:, None] + np.arange(128)[None, :] == 127, BF16)
    counts = lax.dynamic_slice_in_dim(lon_counts, me * band, band)
    counts = jnp.tile(counts, L)[None, :]
    wind = wind_field.transpose(1, 0, 2).reshape(LJ, NX)
    me_arr = me.astype(jnp.int32).reshape(1)
    quad = quad_weights[None, :]
    shapes = (CL, L, C, R, J, W, band)

    vert = vertical.astype(F32).reshape(Z, L, Z, L)

    def vblock(rows, cols):
        v = lax.dynamic_index_in_dim(vert, rows, 0, keepdims=False)
        return lax.dynamic_index_in_dim(v, cols, 1, keepdims=False)

    leg_spec = lambda g0: pl.BlockSpec((R, GROUP, J), lambda g: (0, g + g0, 0))
    low_spec = lambda g0: pl.BlockSpec((GROUP, 128), lambda g: (g + g0, 0))

    gathered = []
    for g0, G in chunks:
        x = own[:, g0 * GROUP : (g0 + G) * GROUP][None]
        if Z == 4:
            pair = [(0, 1), (1, 0), (2, 3), (3, 2)]
            middle = [(1, 2), (2, 1)]
            ends = [(1, 0), (2, 3)]
            a = lax.ppermute(x, "lev", pair)
            b = lax.ppermute(x, "lev", middle)
            c = lax.ppermute(a, "lev", middle)
            table_d = jnp.stack([vblock(z ^ 1, 3 - z), vblock(z ^ 1, (3 - z) ^ 1)])
            spec = pl.BlockSpec((1, CL, GROUP, R), lambda g: (0, 0, g, 0))
            part = pl.pallas_call(
                functools.partial(mix_kernel, L=L, C=C),
                grid=(G,),
                out_shape=jax.ShapeDtypeStruct(x.shape, BF16),
                in_specs=[SMEM, spec, spec],
                out_specs=spec,
                compiler_params=params(),
                name="partial_levels",
            )(table_d, b, c)
            d = lax.ppermute(part, "lev", ends)
            tab = jnp.stack(
                [vblock(z, z), vblock(z, z ^ 1), vblock(z, 3 - z), vblock(z, (3 - z) ^ 1)]
            )
            gathered.append(((x, a, b, c), d, tab))
        else:
            every = lax.all_gather(x, "lev", axis=0, tiled=True)
            tab = lax.dynamic_index_in_dim(vert, z, 0, keepdims=False).transpose(1, 0, 2)
            gathered.append(((every,), None, tab))

    HX = NX // 2
    steps = 5 if rows % 640 == 0 else 1
    per = rows // steps
    bspec = pl.BlockSpec((per, HX), lambda i: (i, 0))
    bases = pl.pallas_call(
        functools.partial(basis_kernel, steps=HX // 128, NX=NX),
        grid=(steps,),
        out_shape=[jax.ShapeDtypeStruct((rows, HX), BF16)] * 2,
        in_specs=[pl.BlockSpec((2, per, 128), lambda i: (0, i, 0))],
        out_specs=[bspec, bspec],
        compiler_params=params(),
        cost_estimate=pl.CostEstimate(
            flops=rows * HX * 8, bytes_accessed=rows * HX * 4, transcendentals=0
        ),
        name="basis",
    )(waves)

    sent = []
    for (g0, G), (srcs, extra, tab) in zip(chunks, gathered):
        specs = [
            pl.BlockSpec((s.shape[0], CL, GROUP, R), lambda g: (0, 0, g, 0)) for s in srcs
        ]
        args = list(srcs)
        if extra is not None:
            specs.append(pl.BlockSpec((1, CL, GROUP, R), lambda g: (0, 0, g, 0)))
            args.append(extra)
        fixed = [me_arr, tab, lows, rep, flip, table, *args]
        shaped = travel_shapes(W, NG, LJ)
        sent = pl.pallas_call(
            functools.partial(
                inverse_kernel, shapes=shapes, n_src=len(srcs), extra=extra is not None
            ),
            grid=(G,),
            out_shape=shaped,
            in_specs=[SMEM, SMEM, low_spec(g0), whole(rep.shape), whole(flip.shape), leg_spec(g0)]
            + specs
            + [pl.BlockSpec(memory_space=pl.ANY)] * len(sent),
            out_specs=[group_spec(v.shape, g0) for v in shaped],
            scratch_shapes=[
                pltpu.VMEM((W, 32, LJ), BF16),
                pltpu.VMEM((CL, GROUP, R), F32),
                pltpu.VMEM((2, CL * 16, R // RBLOCK * RBLOCK * GROUP // 2), BF16),
            ],
            input_output_aliases={len(fixed) + i: i for i in range(len(sent))},
            compiler_params=params(),
            cost_estimate=pl.CostEstimate(
                flops=2 * G * CL * 16 * R * GROUP * J,
                bytes_accessed=G * R * GROUP * J * 2,
                transcendentals=0,
            ),
            name="inverse_legendre",
        )(*fixed, *sent)
    parts = exchange(sent, W)

    XB = 256
    half = HX // XB
    chunks = tuple(pieces(BACK_PIECES, NG))
    shaped = [v for _, G in chunks for v in travel_shapes(W, G, LJ)]
    sent = pl.pallas_call(
        functools.partial(grid_kernel, n_parts=len(parts), W=W, chunks=chunks, NX=NX),
        grid=(half,),
        out_shape=shaped,
        in_specs=[whole(counts.shape)]
        + [whole(p.shape) for p in parts]
        + [pl.BlockSpec((rows, XB), lambda i: (0, i))] * 2
        + [
            whole(waves.shape),
            pl.BlockSpec((LJ, XB), lambda i: (0, i)),
            pl.BlockSpec((LJ, XB), lambda i: (0, i + half)),
        ],
        out_specs=[whole(v.shape) for v in shaped],
        scratch_shapes=[
            pltpu.VMEM((2, rows, LJ), BF16),
            pltpu.VMEM((2, LJ, rows), BF16),
            pltpu.VMEM((2, rows, LJ), F32),
        ],
        compiler_params=params(),
        cost_estimate=pl.CostEstimate(
            flops=4 * rows * LJ * NX, bytes_accessed=2 * NX * (rows + LJ), transcendentals=0
        ),
        name="grid_points",
    )(counts, *parts, *bases, waves, wind, wind)

    out = None
    kinds = len(shaped) // len(chunks)
    arrived = [exchange(sent[i * kinds : (i + 1) * kinds], W) for i in range(len(chunks))]
    for (g0, G), returned in zip(chunks, arrived):
        ospec = pl.BlockSpec((GROUP, C, L, R), lambda g, g0=g0: (g + g0, 0, 0, 0))
        before = [] if out is None else [out]
        fixed = [me_arr, lows, rep, flip, quad, table, *returned]
        out = pl.pallas_call(
            functools.partial(forward_kernel, shapes=shapes, n_parts=len(returned)),
            grid=(G,),
            out_shape=jax.ShapeDtypeStruct((padded, C, L, R), F32),
            in_specs=[
                SMEM, low_spec(g0), whole(rep.shape), whole(flip.shape), whole(quad.shape),
                leg_spec(g0),
            ]
            + [group_spec(p.shape, 0) for p in returned]
            + [pl.BlockSpec(memory_space=pl.ANY)] * len(before),
            out_specs=ospec,
            scratch_shapes=[
                pltpu.VMEM((W, 32, LJ), F32),
                pltpu.VMEM((2, CL * 16, J), BF16),
                pltpu.VMEM((2 * (R // RBLOCK) * CL * GROUP, RBLOCK * GROUP), BF16),
            ],
            input_output_aliases={len(fixed): 0} if before else {},
            compiler_params=params(),
            cost_estimate=pl.CostEstimate(
                flops=2 * G * CL * 16 * R * GROUP * J,
                bytes_accessed=G * R * GROUP * J * 2,
                transcendentals=0,
            ),
            name="forward_legendre",
        )(*fixed, *before)
    return out[:pairs]


def solution(mesh):
    return jax.shard_map(
        shards,
        mesh=mesh,
        in_specs=(
            P("wave", None, "lev", None),
            P("wave", None, None),
            P(),
            P(),
            P(),
            P(),
            P("wave", "lev", None),
        ),
        out_specs=P("wave", None, "lev", None),
        check_vma=False,
    )
```

```python
import functools
import math

import jax
import jax.numpy as jnp
import numpy as np
from jax import lax
from jax.experimental import pallas as pl
from jax.experimental.pallas import tpu as pltpu
from jax.sharding import PartitionSpec as P


GROUP = 8
RBLOCK = 128
F32 = jnp.float32
BF16 = jnp.bfloat16


LEVEL_PIECES = (2, 3)
BACK_PIECES = (3, 2)


def XOR_ORDER(count):
    return count <= 8


def pieces(sizes, count):
    out, at = [], 0
    for size in sizes if sum(sizes) == count else (count,):
        out.append((at, size))
        at += size
    return out


def params(**kw):
    return pltpu.CompilerParams(vmem_limit_bytes=56 * 1024 * 1024, **kw)


def class_masks(low_ref, first_row, count, total):
    shape = (GROUP, count // 2 * GROUP)
    lane = lax.broadcasted_iota(jnp.int32, shape, 1)
    sub = lax.broadcasted_iota(jnp.int32, shape, 0)
    own = (lane & (GROUP - 1)) == sub
    low = low_ref[:, :1]
    masks = []
    for parity in range(2):
        first = (lane >> 3) * 2 + (first_row + parity) < total - low
        wave = jnp.where(first, low, total - 1 - low)
        masks.append([own & ((wave & 1) == s) for s in range(2)])
    return masks


def flipped(low_ref, width):
    return jnp.broadcast_to((low_ref[:, :1] & 1) == 1, (GROUP, width))


def tail_masks(low_ref, total, width):
    wave = jnp.broadcast_to(total - 1 - low_ref[:, :1], (GROUP, width))
    return [(wave & 1) == s for s in range(2)]


def start_table(leg_ref, buf_ref, sem_ref, first):
    g, count = pl.program_id(0), pl.num_programs(0)

    def copy(i, slot):
        source = leg_ref.at[:, pl.ds(pl.multiple_of((first + i) * GROUP, GROUP), GROUP), :]
        return pltpu.make_async_copy(source, buf_ref.at[slot], sem_ref.at[slot])

    @pl.when(g == 0)
    def _():
        copy(0, 0).start()

    @pl.when(g + 1 < count)
    def _():
        copy(g + 1, (g + 1) % 2).start()

    return copy(g, g % 2), buf_ref.at[g % 2]


def mirror(x, flip):
    n, width = x.shape
    tiles = width // 128
    v = jnp.concatenate([x[:, k * 128 : (k + 1) * 128] for k in range(tiles)], axis=0)
    v = jnp.dot(v, flip, preferred_element_type=F32)
    return jnp.concatenate([v[k * n : (k + 1) * n] for k in reversed(range(tiles))], axis=1)


def inverse_kernel(me_ref, vert_ref, low_ref, rep_ref, flip_ref, leg_ref, *rest, shapes, n_src, extra, first):
    CL, L, C, R, J, W, band = shapes
    srcs = rest[:n_src]
    rest = rest[n_src:]
    add_ref = None
    if extra:
        add_ref, rest = rest[0], rest[1:]
    bands_ref, mix_ref, lhs_ref, buf_ref, sem_ref = rest[-5:]
    out_refs = rest[-5 - (W if XOR_ORDER(W) else 1) : -5]
    arriving, leg_ref = start_table(leg_ref, buf_ref, sem_ref, first)
    total = R - 1
    full = R // RBLOCK
    for c in range(C):
        sums = [None] * L
        k = 0
        for src in srcs:
            for s in range(src.shape[0]):
                for li in range(L):
                    x = src[s, c * L + li].astype(F32)
                    for lo in range(L):
                        term = vert_ref[k, lo, li] * x
                        sums[lo] = term if sums[lo] is None else sums[lo] + term
                k += 1
        for lo in range(L):
            v = sums[lo]
            if extra:
                v = v + add_ref[0, c * L + lo].astype(F32)
            mix_ref[c * L + lo] = v.astype(BF16).astype(F32)
    blocks = [
        mix_ref[:, :, b * RBLOCK : (b + 1) * RBLOCK].reshape(CL * GROUP, RBLOCK)
        for b in range(full)
    ]
    spread = jnp.dot(
        jnp.concatenate(blocks, axis=0).astype(BF16), rep_ref[...], preferred_element_type=F32
    )
    width = RBLOCK * GROUP // 2
    for b in range(full):
        masks = class_masks(low_ref, b * RBLOCK, RBLOCK, total)
        for cl in range(CL):
            at = (b * CL + cl) * GROUP
            for parity in range(2):
                x = spread[at : at + GROUP, parity * width : (parity + 1) * width]
                rows = jnp.concatenate(
                    [jnp.where(masks[parity][s], x, 0.0) for s in range(2)], axis=0
                )
                lhs_ref[parity, cl * 16 : (cl + 1) * 16, b * width : (b + 1) * width] = rows.astype(
                    BF16
                )
    arriving.wait()
    table = leg_ref.at[0 : full * RBLOCK].reshape(full * RBLOCK // 2, 2 * GROUP, J)
    kept = []
    for parity in range(2):
        rows = table[:, parity * GROUP : (parity + 1) * GROUP].reshape(full * width, J)
        acc = jnp.dot(lhs_ref[parity], rows, preferred_element_type=F32).reshape(CL, 2, GROUP, J)
        kept.append([[acc[cl, s] for s in range(2)] for cl in range(CL)])
    for r in range(full * RBLOCK, R):
        row = leg_ref[r].astype(F32)
        masks = tail_masks(low_ref, total, J)
        for cl in range(CL):
            term = mix_ref[cl, :, r : r + 1] * row
            for s in range(2):
                kept[r % 2][cl][s] = kept[r % 2][cl][s] + jnp.where(masks[s], term, 0.0)
    flips = flipped(low_ref, J)
    north, south = [], []
    for cl in range(CL):
        even, odd = kept[0][cl], kept[1][cl]
        north.append([even[s] + odd[s] for s in range(2)])
        less = [even[s] - odd[s] for s in range(2)]
        south += [jnp.where(flips, -less[0], less[0]), less[1]]
    south = mirror(jnp.concatenate(south, axis=0).astype(BF16), flip_ref[...])
    half = W // 2
    for w in range(W):
        lo = (w % half) * band
        for s in range(2):
            both = []
            for c in range(C):
                pieces = []
                for l in range(L):
                    cl = c * L + l
                    at = cl * 16 + s * GROUP
                    v = north[cl][s] if w < half else south[at : at + GROUP]
                    pieces.append(v[:, lo : lo + band])
                both.append(jnp.concatenate(pieces, axis=1))
            bands_ref[w, s * 16 : (s + 1) * 16, :] = jnp.concatenate(both, axis=0).astype(BF16)
    if XOR_ORDER(W):
        for d in range(W):
            out_refs[d][0] = bands_ref[me_ref[0] ^ d]
    else:
        out_refs[0][:, 0] = bands_ref[...]


def mix_kernel(vert_ref, *rest, L, C):
    srcs, out_ref = rest[:-1], rest[-1]
    for c in range(C):
        sums = [None] * L
        for k, src in enumerate(srcs):
            for li in range(L):
                x = src[0, c * L + li].astype(F32)
                for lo in range(L):
                    term = vert_ref[k, lo, li] * x
                    sums[lo] = term if sums[lo] is None else sums[lo] + term
        for lo in range(L):
            out_ref[0, c * L + lo] = sums[lo].astype(BF16)


def turn(phase, period):
    x = phase.astype(F32) * (4.0 / period)
    quarter = jnp.floor(x + 0.5)
    y = phase.astype(F32) - quarter * (period / 4)
    y = y * (2.0 * math.pi / period)
    z = y * y
    s = y * (1.0 + z * (-1.0 / 6 + z * (1.0 / 120 + z * (-1.0 / 5040 + z * (1.0 / 362880)))))
    c = 1.0 + z * (-0.5 + z * (1.0 / 24 + z * (-1.0 / 720 + z * (1.0 / 40320))))
    k = quarter.astype(jnp.int32)
    swap = (k & 1) == 1
    cos = jnp.where(swap, s, c)
    sin = jnp.where(swap, c, s)
    cos = jnp.where(((k + 1) & 2) == 2, -cos, cos)
    sin = jnp.where((k & 2) == 2, -sin, sin)
    return cos, sin


def basis_kernel(wave_ref, even_ref, odd_ref, *, steps, NX):
    lane = lax.broadcasted_iota(jnp.int32, (1, 1, 128), 2)
    for k, ref in enumerate((even_ref, odd_ref)):
        m = wave_ref[k].reshape(-1, 2, GROUP, 128)[:, 0]
        c, s = turn(m * lane, NX)
        dc, ds = turn(m * 128, NX)
        factor = jnp.where(m == 0, 1.0, 2.0)
        c, s = c * factor, s * factor
        for a in range(steps):
            v = jnp.concatenate([c, -s], axis=1).astype(BF16)
            ref[:, a * 128 : (a + 1) * 128] = v.reshape(-1, 128)
            c, s = c * dc - s * ds, s * dc + c * ds


def grid_kernel(counts_ref, *rest, n_parts, W, chunks, NX):
    parts = rest[:n_parts]
    even_ref, odd_ref, wave_ref, near_ref, far_ref = rest[n_parts : n_parts + 5]
    out_refs = rest[n_parts + 5 : -3]
    flat_ref, turned_ref, back_ref = rest[-3:]
    rows = flat_ref.shape[1]
    LJ = counts_ref.shape[1]
    step = pl.program_id(0)

    @pl.when(step == 0)
    def _():
        at = 0
        for part in parts:
            many = len(part.shape) == 4
            for i in range(part.shape[0] if many else 1):
                for g in range(part.shape[-3]):
                    to = (g * W + at) * 16
                    v = part[i, g] if many else part[g]
                    for s in range(2):
                        flat_ref[s, to : to + 16, :] = v[s * 16 : (s + 1) * 16]
                at += 1
        for s in range(2):
            for lo in range(0, rows, 128):
                hi = min(lo + 128, rows)
                keep = 2 * wave_ref[s, lo:hi, :1] < counts_ref[...]
                v = jnp.where(keep, flat_ref[s, lo:hi, :].astype(F32), 0.0).astype(BF16)
                turned_ref[s, :, lo:hi] = v.T
        back_ref[...] = jnp.zeros_like(back_ref)

    bases = (even_ref, odd_ref)
    even = jnp.dot(turned_ref[0], even_ref[...], preferred_element_type=F32)
    odd = jnp.dot(turned_ref[1], odd_ref[...], preferred_element_type=F32)
    near = near_ref[...] * (even + odd).astype(BF16)
    far = far_ref[...] * (even - odd).astype(BF16)
    for s, forcing in enumerate((near + far, near - far)):
        back_ref[s] += lax.dot_general(
            bases[s][...], forcing, (((1,), (1,)), ((), ())), preferred_element_type=F32
        )

    @pl.when(step == pl.num_programs(0) - 1)
    def _():
        for s in range(2):
            m = wave_ref[s][:, :1]
            scale = jnp.where(m == 0, 1.0 / NX, 0.5 / NX)
            v = jnp.where(2 * m < counts_ref[...], back_ref[s] * scale, 0.0).astype(BF16)
            k = 0
            for g0, G in chunks:
                for d in range(W):
                    for g in range(G):
                        at = ((g0 + g) * W + d) * 16
                        if XOR_ORDER(W):
                            out_refs[k + d][g, s * 16 : (s + 1) * 16, :] = v[at : at + 16]
                        else:
                            out_refs[k][d, g, s * 16 : (s + 1) * 16, :] = v[at : at + 16]
                k += W if XOR_ORDER(W) else 1


def forward_kernel(me_ref, low_ref, rep_ref, flip_ref, quad_ref, leg_ref, *rest, shapes, n_parts, first):
    CL, L, C, R, J, W, band = shapes
    parts = rest[:n_parts]
    out_ref, bands_ref, fold_ref, kept_ref, buf_ref, sem_ref = rest[-6:]
    arriving, leg_ref = start_table(leg_ref, buf_ref, sem_ref, first)
    total = R - 1
    full = R // RBLOCK
    half = W // 2
    k = 0
    for part in parts:
        many = len(part.shape) == 4
        for i in range(part.shape[0] if many else 1):
            slot = me_ref[0] ^ k if XOR_ORDER(W) else k
            bands_ref[slot] = (part[i, 0] if many else part[0]).astype(F32)
            k += 1
    quad = quad_ref[...]
    norths, souths = [], []
    for l in range(L):
        cut = slice(l * band, (l + 1) * band)
        norths.append(jnp.concatenate([bands_ref[w, :, cut] for w in range(half)], axis=1))
        souths.append(jnp.concatenate([bands_ref[w, :, cut] for w in range(half, W)], axis=1))
    souths = mirror(jnp.concatenate(souths, axis=0).astype(BF16), flip_ref[...])
    flips = flipped(low_ref, J)
    for l in range(L):
        south = souths[l * 32 : (l + 1) * 32]
        even = (norths[l] + south) * quad
        odd = (norths[l] - south) * quad
        for c in range(C):
            at = (c * L + l) * 16
            for parity, (v, u) in enumerate(((even, odd), (odd, even))):
                lo, hi = c * GROUP, 16 + c * GROUP
                first = jnp.where(flips, u[lo : lo + GROUP], v[lo : lo + GROUP])
                rows = jnp.concatenate([first, v[hi : hi + GROUP]], axis=0)
                fold_ref[parity, at : at + 16, :] = rows.astype(BF16)
    width = RBLOCK * GROUP // 2
    n = CL * GROUP
    arriving.wait()
    table = leg_ref.at[0 : full * RBLOCK].reshape(full * RBLOCK // 2, 2 * GROUP, J)
    for parity in range(2):
        rows = table[:, parity * GROUP : (parity + 1) * GROUP].reshape(full * width, J)
        res = lax.dot_general(
            fold_ref[parity], rows, (((1,), (1,)), ((), ())), preferred_element_type=F32
        )
        for b in range(full):
            masks = class_masks(low_ref, b * RBLOCK, RBLOCK, total)[parity]
            for cl in range(0, CL, 2):
                pair = []
                for i in range(cl, cl + 2):
                    own = [
                        res[i * 16 + s * GROUP : i * 16 + (s + 1) * GROUP, b * width : (b + 1) * width]
                        for s in range(2)
                    ]
                    v = jnp.where(masks[0], own[0], jnp.where(masks[1], own[1], 0.0))
                    pair.append(v)
                v = jnp.concatenate(pair, axis=0)
                high = v.astype(BF16)
                at = b * n + cl * GROUP
                cut = slice(parity * width, (parity + 1) * width)
                kept_ref[at : at + 16, cut] = high
                kept_ref[full * n + at : full * n + at + 16, cut] = (v - high.astype(F32)).astype(BF16)
    packed = lax.dot_general(
        kept_ref[...], rep_ref[...], (((1,), (1,)), ((), ())), preferred_element_type=F32
    )
    packed = packed[: full * n] + packed[full * n :]
    for b in range(full):
        v = jnp.swapaxes(packed[b * n : (b + 1) * n].reshape(CL, GROUP, RBLOCK), 0, 1)
        for c in range(C):
            out_ref[:, c, :, b * RBLOCK : (b + 1) * RBLOCK] = v[:, c * L : (c + 1) * L]
    for r in range(full * RBLOCK, R):
        row = leg_ref[r].astype(F32)
        masks = tail_masks(low_ref, total, J)
        for cl in range(CL):
            rows = fold_ref[r % 2, cl * 16 : (cl + 1) * 16, :].astype(F32)
            v = jnp.where(masks[0], rows[:GROUP], jnp.where(masks[1], rows[GROUP:], 0.0))
            v = jnp.sum(v * row, axis=1, keepdims=True)
            out_ref[:, cl // L, cl % L, r : r + 1] = v


def whole(shape):
    return pl.BlockSpec(shape, lambda *_: (0,) * len(shape))


SMEM = pl.BlockSpec(memory_space=pltpu.SMEM)


def exchange(sent, count):
    if not XOR_ORDER(count):
        return [lax.all_to_all(sent[0], "wave", 0, 0, tiled=True)]
    parts = [sent[0]]
    for d in range(1, count):
        parts.append(lax.ppermute(sent[d], "wave", [(i, i ^ d) for i in range(count)]))
    return parts


def travel_shapes(W, groups, width):
    if XOR_ORDER(W):
        return [jax.ShapeDtypeStruct((groups, 32, width), BF16)] * W
    return [jax.ShapeDtypeStruct((W, groups, 32, width), BF16)]


def group_spec(shape, first):
    if len(shape) == 3:
        return pl.BlockSpec((1,) + shape[1:], lambda g: (g + first, 0, 0))
    return pl.BlockSpec((shape[0], 1) + shape[2:], lambda g: (0, g + first, 0, 0))


def shards(spectral, legendre, quad_weights, pair_order, lon_counts, vertical, wind_field):
    W, Z = lax.axis_size("wave"), lax.axis_size("lev")
    pairs, C, L, R = spectral.shape
    J = legendre.shape[2]
    band, NX = wind_field.shape[0], wind_field.shape[2]
    CL, LJ, total = C * L, L * band, R - 1
    me, z = lax.axis_index("wave"), lax.axis_index("lev")
    padded = -(-pairs // GROUP) * GROUP
    NG = padded // GROUP
    chunks = pieces(LEVEL_PIECES, NG)
    pads = padded - pairs

    own = spectral.transpose(1, 2, 0, 3).reshape(CL, pairs, R)
    own = jnp.pad(own, ((0, 0), (0, pads), (0, 0)))
    table = jnp.pad(legendre.transpose(1, 0, 2), ((0, 0), (0, pads), (0, 0)))

    own_pairs = pair_order.reshape(W, pairs)
    all_pairs = jnp.pad(own_pairs, ((0, 0), (0, pads)))
    lows = lax.dynamic_index_in_dim(all_pairs, me, 0, keepdims=False)
    lows = jnp.broadcast_to(lows[:, None], (padded, 128))
    if XOR_ORDER(W):
        all_pairs = all_pairs[me ^ jnp.arange(W)]
    all_pairs = all_pairs.reshape(W, NG, 1, GROUP)
    others = total - 1 - all_pairs
    is_odd = (all_pairs & 1) == 1
    evens = jnp.where(is_odd, others, all_pairs)
    waves = jnp.stack([evens, total - 1 - evens]).transpose(0, 2, 1, 3, 4)
    rows = NG * W * 16
    waves = jnp.broadcast_to(waves, (2, NG, W, 2, GROUP)).reshape(2, rows, 1)
    waves = jnp.broadcast_to(waves, (2, rows, 128))

    lane = np.arange(RBLOCK * GROUP)[None, :]
    half_width = RBLOCK * GROUP // 2
    rep = np.arange(RBLOCK)[:, None] == lane % half_width // GROUP * 2 + lane // half_width
    rep = jnp.asarray(rep, BF16)
    flip = jnp.asarray(np.arange(128)[:, None] + np.arange(128)[None, :] == 127, BF16)
    counts = lax.dynamic_slice_in_dim(lon_counts, me * band, band)
    counts = jnp.tile(counts, L)[None, :]
    wind = wind_field.transpose(1, 0, 2).reshape(LJ, NX)
    me_arr = me.astype(jnp.int32).reshape(1)
    quad = quad_weights[None, :]
    shapes = (CL, L, C, R, J, W, band)

    vert = vertical.astype(F32).reshape(Z, L, Z, L)

    def vblock(rows, cols):
        v = lax.dynamic_index_in_dim(vert, rows, 0, keepdims=False)
        return lax.dynamic_index_in_dim(v, cols, 1, keepdims=False)

    leg_spec = pl.BlockSpec(memory_space=pl.ANY)
    leg_scratch = [pltpu.VMEM((2, R, GROUP, J), BF16), pltpu.SemaphoreType.DMA((2,))]
    low_spec = lambda g0: pl.BlockSpec((GROUP, 128), lambda g: (g + g0, 0))

    gathered = []
    for g0, G in chunks:
        x = own[:, g0 * GROUP : (g0 + G) * GROUP][None]
        if Z == 4:
            a = lax.ppermute(x, "lev", [(i, i ^ 1) for i in range(4)])
            table_d = jnp.stack([vblock(z ^ 2, z), vblock(z ^ 2, z ^ 1)])
            spec = pl.BlockSpec((1, CL, GROUP, R), lambda g: (0, 0, g, 0))
            part = pl.pallas_call(
                functools.partial(mix_kernel, L=L, C=C),
                grid=(G,),
                out_shape=jax.ShapeDtypeStruct(x.shape, BF16),
                in_specs=[SMEM, spec, spec],
                out_specs=spec,
                compiler_params=params(),
                name="partial_levels",
            )(table_d, x, a)
            d = lax.ppermute(part, "lev", [(i, i ^ 2) for i in range(4)])
            gathered.append(((x, a), d, jnp.stack([vblock(z, z), vblock(z, z ^ 1)])))
        else:
            every = lax.all_gather(x, "lev", axis=0, tiled=True)
            tab = lax.dynamic_index_in_dim(vert, z, 0, keepdims=False).transpose(1, 0, 2)
            gathered.append(((every,), None, tab))

    HX = NX // 2
    steps = 5 if rows % 640 == 0 else 1
    per = rows // steps
    bspec = pl.BlockSpec((per, HX), lambda i: (i, 0))
    bases = pl.pallas_call(
        functools.partial(basis_kernel, steps=HX // 128, NX=NX),
        grid=(steps,),
        out_shape=[jax.ShapeDtypeStruct((rows, HX), BF16)] * 2,
        in_specs=[pl.BlockSpec((2, per, 128), lambda i: (0, i, 0))],
        out_specs=[bspec, bspec],
        compiler_params=params(),
        cost_estimate=pl.CostEstimate(
            flops=rows * HX * 8, bytes_accessed=rows * HX * 4, transcendentals=0
        ),
        name="basis",
    )(waves)

    sent = []
    for (g0, G), (srcs, extra, tab) in zip(chunks, gathered):
        specs = [
            pl.BlockSpec((s.shape[0], CL, GROUP, R), lambda g: (0, 0, g, 0)) for s in srcs
        ]
        args = list(srcs)
        if extra is not None:
            specs.append(pl.BlockSpec((1, CL, GROUP, R), lambda g: (0, 0, g, 0)))
            args.append(extra)
        fixed = [me_arr, tab, lows, rep, flip, table, *args]
        shaped = travel_shapes(W, NG, LJ)
        sent = pl.pallas_call(
            functools.partial(
                inverse_kernel, shapes=shapes, n_src=len(srcs), extra=extra is not None, first=g0
            ),
            grid=(G,),
            out_shape=shaped,
            in_specs=[SMEM, SMEM, low_spec(g0), whole(rep.shape), whole(flip.shape), leg_spec]
            + specs
            + [pl.BlockSpec(memory_space=pl.ANY)] * len(sent),
            out_specs=[group_spec(v.shape, g0) for v in shaped],
            scratch_shapes=[
                pltpu.VMEM((W, 32, LJ), BF16),
                pltpu.VMEM((CL, GROUP, R), F32),
                pltpu.VMEM((2, CL * 16, R // RBLOCK * RBLOCK * GROUP // 2), BF16),
            ]
            + leg_scratch,
            input_output_aliases={len(fixed) + i: i for i in range(len(sent))},
            compiler_params=params(),
            cost_estimate=pl.CostEstimate(
                flops=2 * G * CL * 16 * R * GROUP * J,
                bytes_accessed=G * R * GROUP * J * 2,
                transcendentals=0,
            ),
            name="inverse_legendre",
        )(*fixed, *sent)
    parts = exchange(sent, W)

    XB = 256
    half = HX // XB
    chunks = tuple(pieces(BACK_PIECES, NG))
    shaped = [v for _, G in chunks for v in travel_shapes(W, G, LJ)]
    sent = pl.pallas_call(
        functools.partial(grid_kernel, n_parts=len(parts), W=W, chunks=chunks, NX=NX),
        grid=(half,),
        out_shape=shaped,
        in_specs=[whole(counts.shape)]
        + [whole(p.shape) for p in parts]
        + [pl.BlockSpec((rows, XB), lambda i: (0, i))] * 2
        + [
            whole(waves.shape),
            pl.BlockSpec((LJ, XB), lambda i: (0, i)),
            pl.BlockSpec((LJ, XB), lambda i: (0, i + half)),
        ],
        out_specs=[whole(v.shape) for v in shaped],
        scratch_shapes=[
            pltpu.VMEM((2, rows, LJ), BF16),
            pltpu.VMEM((2, LJ, rows), BF16),
            pltpu.VMEM((2, rows, LJ), F32),
        ],
        compiler_params=params(),
        cost_estimate=pl.CostEstimate(
            flops=4 * rows * LJ * NX, bytes_accessed=2 * NX * (rows + LJ), transcendentals=0
        ),
        name="grid_points",
    )(counts, *parts, *bases, waves, wind, wind)

    out = None
    kinds = len(shaped) // len(chunks)
    arrived = [exchange(sent[i * kinds : (i + 1) * kinds], W) for i in range(len(chunks))]
    for (g0, G), returned in zip(chunks, arrived):
        ospec = pl.BlockSpec((GROUP, C, L, R), lambda g, g0=g0: (g + g0, 0, 0, 0))
        before = [] if out is None else [out]
        fixed = [me_arr, lows, rep, flip, quad, table, *returned]
        out = pl.pallas_call(
            functools.partial(
                forward_kernel, shapes=shapes, n_parts=len(returned), first=g0
            ),
            grid=(G,),
            out_shape=jax.ShapeDtypeStruct((padded, C, L, R), F32),
            in_specs=[
                SMEM, low_spec(g0), whole(rep.shape), whole(flip.shape), whole(quad.shape),
                leg_spec,
            ]
            + [group_spec(p.shape, 0) for p in returned]
            + [pl.BlockSpec(memory_space=pl.ANY)] * len(before),
            out_specs=ospec,
            scratch_shapes=[
                pltpu.VMEM((W, 32, LJ), F32),
                pltpu.VMEM((2, CL * 16, J), BF16),
                pltpu.VMEM((2 * (R // RBLOCK) * CL * GROUP, RBLOCK * GROUP), BF16),
            ]
            + leg_scratch,
            input_output_aliases={len(fixed): 0} if before else {},
            compiler_params=params(),
            cost_estimate=pl.CostEstimate(
                flops=2 * G * CL * 16 * R * GROUP * J,
                bytes_accessed=G * R * GROUP * J * 2,
                transcendentals=0,
            ),
            name="forward_legendre",
        )(*fixed, *before)
    return out[:pairs]


def solution(mesh):
    return jax.shard_map(
        shards,
        mesh=mesh,
        in_specs=(
            P("wave", None, "lev", None),
            P("wave", None, None),
            P(),
            P(),
            P(),
            P(),
            P("wave", "lev", None),
        ),
        out_specs=P("wave", None, "lev", None),
        check_vma=False,
    )
```

```python
import functools
import math

import jax
import jax.numpy as jnp
import numpy as np
from jax import lax
from jax.experimental import pallas as pl
from jax.experimental.pallas import tpu as pltpu
from jax.sharding import PartitionSpec as P


VMEM_LIMIT = 56 * 1024 * 1024
GROUP = 8
RBLOCK = 128
TABLE_CUTS = (256,)
F32 = jnp.float32
BF16 = jnp.bfloat16


EARLY = True
NATIVE_BACK = False
NATIVE = True
AFTER = 1
LEVEL_PIECES = (2, 3)
BACK_PIECES = (3, 2)


def XOR_ORDER(count):
    return count <= 8


def pieces(sizes, count):
    out, at = [], 0
    for size in sizes if sum(sizes) == count else (count,):
        out.append((at, size))
        at += size
    return out


def params(**kw):
    return pltpu.CompilerParams(vmem_limit_bytes=VMEM_LIMIT, **kw)


def class_masks(low_ref, first_row, count, total):
    shape = (GROUP, count // 2 * GROUP)
    lane = lax.broadcasted_iota(jnp.int32, shape, 1)
    sub = lax.broadcasted_iota(jnp.int32, shape, 0)
    own = (lane & (GROUP - 1)) == sub
    low = low_ref[:, :1]
    masks = []
    for parity in range(2):
        first = (lane >> 3) * 2 + (first_row + parity) < total - low
        wave = jnp.where(first, low, total - 1 - low)
        masks.append([own & ((wave & 1) == s) for s in range(2)])
    return masks


def flipped(low_ref, width):
    return jnp.broadcast_to((low_ref[:, :1] & 1) == 1, (GROUP, width))


def tail_masks(low_ref, total, width):
    wave = jnp.broadcast_to(total - 1 - low_ref[:, :1], (GROUP, width))
    return [(wave & 1) == s for s in range(2)]


def start_table(leg_ref, buf_ref, sem_ref, first):
    g, count = pl.program_id(0), pl.num_programs(0)
    R = leg_ref.shape[0]
    cuts = [0, *TABLE_CUTS, R]

    def copies(i, slot):
        at = pl.multiple_of((first + i) * GROUP, GROUP)
        out = []
        for k, (lo, hi) in enumerate(zip(cuts[:-1], cuts[1:])):
            source = leg_ref.at[lo:hi, pl.ds(at, GROUP), :]
            target = buf_ref.at[slot, lo:hi]
            out.append(pltpu.make_async_copy(source, target, sem_ref.at[slot, k]))
        return out

    @pl.when(g == 0)
    def _():
        for copy in copies(0, 0):
            copy.start()

    @pl.when(g + 1 < count)
    def _():
        for copy in copies(g + 1, (g + 1) % 2):
            copy.start()

    return copies(g, g % 2), buf_ref.at[g % 2]


def mirror(x, flip):
    n, width = x.shape
    tiles = width // 128
    v = jnp.concatenate([x[:, k * 128 : (k + 1) * 128] for k in range(tiles)], axis=0)
    v = jnp.dot(v, flip, preferred_element_type=F32)
    return jnp.concatenate([v[k * n : (k + 1) * n] for k in reversed(range(tiles))], axis=1)


def inverse_kernel(me_ref, vert_ref, low_ref, rep_ref, flip_ref, leg_ref, *rest, shapes, n_src, extra, first, n_out):
    CL, L, C, R, J, W, band = shapes
    srcs = rest[:n_src]
    rest = rest[n_src:]
    add_ref = None
    if extra:
        add_ref, rest = rest[0], rest[1:]
    bands_ref, mix_ref, lhs_ref, buf_ref, sem_ref = rest[-5:]
    out_refs = rest[-5 - n_out : -5]
    arriving, leg_ref = start_table(leg_ref, buf_ref, sem_ref, first)
    total = R - 1
    full = R // RBLOCK
    for c in range(C):
        sums = [None] * L
        k = 0
        for src in srcs:
            for s in range(src.shape[0]):
                for li in range(L):
                    x = src[s, c * L + li].astype(F32)
                    for lo in range(L):
                        term = vert_ref[k, lo, li] * x
                        sums[lo] = term if sums[lo] is None else sums[lo] + term
                k += 1
        for lo in range(L):
            v = sums[lo]
            if extra:
                v = v + add_ref[0, c * L + lo].astype(F32)
            mix_ref[c * L + lo] = v.astype(BF16).astype(F32)
    blocks = [
        mix_ref[:, :, b * RBLOCK : (b + 1) * RBLOCK].reshape(CL * GROUP, RBLOCK)
        for b in range(full)
    ]
    spread = jnp.dot(
        jnp.concatenate(blocks, axis=0).astype(BF16), rep_ref[...], preferred_element_type=F32
    )
    width = RBLOCK * GROUP // 2
    for b in range(full):
        masks = class_masks(low_ref, b * RBLOCK, RBLOCK, total)
        for cl in range(CL):
            at = (b * CL + cl) * GROUP
            for parity in range(2):
                x = spread[at : at + GROUP, parity * width : (parity + 1) * width]
                rows = jnp.concatenate(
                    [jnp.where(masks[parity][s], x, 0.0) for s in range(2)], axis=0
                )
                lhs_ref[parity, cl * 16 : (cl + 1) * 16, b * width : (b + 1) * width] = rows.astype(
                    BF16
                )
    sums = [None, None]
    edges = [0, *TABLE_CUTS, full * RBLOCK]
    for copy, lo, hi in zip(arriving, edges[:-1], edges[1:]):
        copy.wait()
        table = leg_ref.at[lo:hi].reshape((hi - lo) // 2, 2 * GROUP, J)
        for parity in range(2):
            rows = table[:, parity * GROUP : (parity + 1) * GROUP].reshape((hi - lo) // 2 * GROUP, J)
            left = lhs_ref[parity, :, lo // 2 * GROUP : hi // 2 * GROUP]
            v = jnp.dot(left, rows, preferred_element_type=F32)
            sums[parity] = v if sums[parity] is None else sums[parity] + v
    kept = []
    for acc in sums:
        acc = acc.reshape(CL, 2, GROUP, J)
        kept.append([[acc[cl, s] for s in range(2)] for cl in range(CL)])
    for r in range(full * RBLOCK, R):
        row = leg_ref[r].astype(F32)
        masks = tail_masks(low_ref, total, J)
        for cl in range(CL):
            term = mix_ref[cl, :, r : r + 1] * row
            for s in range(2):
                kept[r % 2][cl][s] = kept[r % 2][cl][s] + jnp.where(masks[s], term, 0.0)
    flips = flipped(low_ref, J)
    north, south = [], []
    for cl in range(CL):
        even, odd = kept[0][cl], kept[1][cl]
        north.append([even[s] + odd[s] for s in range(2)])
        less = [even[s] - odd[s] for s in range(2)]
        south += [jnp.where(flips, -less[0], less[0]), less[1]]
    south = mirror(jnp.concatenate(south, axis=0).astype(BF16), flip_ref[...])
    half = W // 2
    for w in range(W):
        lo = (w % half) * band
        for s in range(2):
            both = []
            for c in range(C):
                pieces = []
                for l in range(L):
                    cl = c * L + l
                    at = cl * 16 + s * GROUP
                    v = north[cl][s] if w < half else south[at : at + GROUP]
                    pieces.append(v[:, lo : lo + band])
                both.append(jnp.concatenate(pieces, axis=1))
            bands_ref[w, s * 16 : (s + 1) * 16, :] = jnp.concatenate(both, axis=0).astype(BF16)
    if n_out > 1:
        for d in range(W):
            out_refs[d][0] = bands_ref[me_ref[0] ^ d]
    else:
        out_refs[0][:, 0] = bands_ref[...]


def mix_kernel(vert_ref, *rest, L, C):
    srcs, out_ref = rest[:-1], rest[-1]
    for c in range(C):
        sums = [None] * L
        for k, src in enumerate(srcs):
            for li in range(L):
                x = src[0, c * L + li].astype(F32)
                for lo in range(L):
                    term = vert_ref[k, lo, li] * x
                    sums[lo] = term if sums[lo] is None else sums[lo] + term
        for lo in range(L):
            out_ref[0, c * L + lo] = sums[lo].astype(out_ref.dtype)


def turn(phase, period):
    x = phase.astype(F32) * (4.0 / period)
    quarter = jnp.floor(x + 0.5)
    y = phase.astype(F32) - quarter * (period / 4)
    y = y * (2.0 * math.pi / period)
    z = y * y
    s = y * (1.0 + z * (-1.0 / 6 + z * (1.0 / 120 + z * (-1.0 / 5040 + z * (1.0 / 362880)))))
    c = 1.0 + z * (-0.5 + z * (1.0 / 24 + z * (-1.0 / 720 + z * (1.0 / 40320))))
    k = quarter.astype(jnp.int32)
    swap = (k & 1) == 1
    cos = jnp.where(swap, s, c)
    sin = jnp.where(swap, c, s)
    cos = jnp.where(((k + 1) & 2) == 2, -cos, cos)
    sin = jnp.where((k & 2) == 2, -sin, sin)
    return cos, sin


def basis_kernel(wave_ref, even_ref, odd_ref, *, steps, NX):
    lane = lax.broadcasted_iota(jnp.int32, (1, 1, 128), 2)
    for k, ref in enumerate((even_ref, odd_ref)):
        m = wave_ref[k].reshape(-1, 2, GROUP, 128)[:, 0]
        c, s = turn(m * lane, NX)
        c64, s64 = c[..., 64:65], s[..., 64:65]
        dc = jnp.broadcast_to(1.0 - 2.0 * s64 * s64, c.shape)
        ds = jnp.broadcast_to(2.0 * s64 * c64, c.shape)
        factor = jnp.where(m == 0, 1.0, 2.0)
        c, s = c * factor, s * factor
        for a in range(steps):
            v = jnp.concatenate([c, -s], axis=1).astype(BF16)
            ref[:, a * 128 : (a + 1) * 128] = v.reshape(-1, 128)
            c, s = c * dc - s * ds, s * dc + c * ds


def wide(x, width):
    if width % 128:
        return jnp.broadcast_to(x[:, :1], (x.shape[0], width))
    return jnp.concatenate([x] * (width // 128), axis=1)


def grid_kernel(me_ref, counts_ref, *rest, places, W, chunks, counts_out, NX):
    n_parts = len(places)
    parts = rest[:n_parts]
    even_ref, odd_ref, wave_ref, near_ref, far_ref = rest[n_parts : n_parts + 5]
    out_refs = rest[n_parts + 5 : -3]
    flat_ref, turned_ref, back_ref = rest[-3:]
    rows = flat_ref.shape[1]
    LJ = counts_ref.shape[1]
    step = pl.program_id(0)

    @pl.when(step == 0)
    def _():
        for part, (g0, d) in zip(parts, places):
            many = len(part.shape) == 4
            for i in range(part.shape[0] if many else 1):
                slot = d
                if many:
                    slot = me_ref[0] ^ i if XOR_ORDER(W) else i
                for g in range(part.shape[-3]):
                    to = ((g0 + g) * W + slot) * 16
                    if many:
                        to = pl.multiple_of(to, 16)
                    v = part[i, g] if many else part[g]
                    for s in range(2):
                        flat_ref[s, pl.ds(to, 16), :] = v[s * 16 : (s + 1) * 16]
        for s in range(2):
            for lo in range(0, rows, 128):
                hi = min(lo + 128, rows)
                keep = wide(2 * wave_ref[s, lo:hi], LJ) < counts_ref[...]
                v = jnp.where(keep, flat_ref[s, lo:hi, :].astype(F32), 0.0).astype(BF16)
                turned_ref[s, :, lo:hi] = v.T
        back_ref[...] = jnp.zeros_like(back_ref)

    bases = (even_ref, odd_ref)
    even = jnp.dot(turned_ref[0], even_ref[...], preferred_element_type=F32)
    odd = jnp.dot(turned_ref[1], odd_ref[...], preferred_element_type=F32)
    near = near_ref[...] * (even + odd).astype(BF16)
    far = far_ref[...] * (even - odd).astype(BF16)
    for s, forcing in enumerate((near + far, near - far)):
        back_ref[s] += lax.dot_general(
            bases[s][...], forcing, (((1,), (1,)), ((), ())), preferred_element_type=F32
        )

    @pl.when(step == pl.num_programs(0) - 1)
    def _():
        for s in range(2):
            m = wave_ref[s]
            scale = wide(jnp.where(m == 0, 1.0 / NX, 0.5 / NX), LJ)
            keep = wide(2 * m, LJ) < counts_ref[...]
            v = jnp.where(keep, back_ref[s] * scale, 0.0).astype(BF16)
            k = 0
            for (g0, G), count in zip(chunks, counts_out):
                for d in range(W):
                    for g in range(G):
                        at = ((g0 + g) * W + d) * 16
                        if count > 1:
                            out_refs[k + d][g, s * 16 : (s + 1) * 16, :] = v[at : at + 16]
                        else:
                            to = me_ref[0] ^ d if XOR_ORDER(W) else d
                            out_refs[k][to, g, s * 16 : (s + 1) * 16, :] = v[at : at + 16]
                k += count


def forward_kernel(me_ref, low_ref, rep_ref, flip_ref, quad_ref, leg_ref, *rest, shapes, n_parts, first):
    CL, L, C, R, J, W, band = shapes
    parts = rest[:n_parts]
    out_ref, bands_ref, fold_ref, kept_ref, buf_ref, sem_ref = rest[-6:]
    arriving, leg_ref = start_table(leg_ref, buf_ref, sem_ref, first)
    total = R - 1
    full = R // RBLOCK
    half = W // 2
    k = 0
    for part in parts:
        many = len(part.shape) == 4
        for i in range(part.shape[0] if many else 1):
            slot = i if many else me_ref[0] ^ k
            bands_ref[slot] = (part[i, 0] if many else part[0]).astype(F32)
            k += 1
    quad = quad_ref[...]
    norths, souths = [], []
    for l in range(L):
        cut = slice(l * band, (l + 1) * band)
        norths.append(jnp.concatenate([bands_ref[w, :, cut] for w in range(half)], axis=1))
        souths.append(jnp.concatenate([bands_ref[w, :, cut] for w in range(half, W)], axis=1))
    souths = mirror(jnp.concatenate(souths, axis=0).astype(BF16), flip_ref[...])
    flips = flipped(low_ref, J)
    for l in range(L):
        south = souths[l * 32 : (l + 1) * 32]
        even = (norths[l] + south) * quad
        odd = (norths[l] - south) * quad
        for c in range(C):
            at = (c * L + l) * 16
            for parity, (v, u) in enumerate(((even, odd), (odd, even))):
                lo, hi = c * GROUP, 16 + c * GROUP
                first = jnp.where(flips, u[lo : lo + GROUP], v[lo : lo + GROUP])
                rows = jnp.concatenate([first, v[hi : hi + GROUP]], axis=0)
                fold_ref[parity, at : at + 16, :] = rows.astype(BF16)
    width = RBLOCK * GROUP // 2
    n = CL * GROUP
    edges = [0, *TABLE_CUTS, full * RBLOCK]
    for copy, first_row, last_row in zip(arriving, edges[:-1], edges[1:]):
        copy.wait()
        table = leg_ref.at[first_row:last_row].reshape((last_row - first_row) // 2, 2 * GROUP, J)
        for parity in range(2):
            rows = table[:, parity * GROUP : (parity + 1) * GROUP].reshape(-1, J)
            res = lax.dot_general(
                fold_ref[parity], rows, (((1,), (1,)), ((), ())), preferred_element_type=F32
            )
            for b in range(first_row // RBLOCK, last_row // RBLOCK):
                masks = class_masks(low_ref, b * RBLOCK, RBLOCK, total)[parity]
                here = (b - first_row // RBLOCK) * width
                for cl in range(0, CL, 2):
                    pair = []
                    for i in range(cl, cl + 2):
                        own = [
                            res[
                                i * 16 + s * GROUP : i * 16 + (s + 1) * GROUP, here : here + width
                            ]
                            for s in range(2)
                        ]
                        v = jnp.where(masks[0], own[0], jnp.where(masks[1], own[1], 0.0))
                        pair.append(v)
                    v = jnp.concatenate(pair, axis=0)
                    high = v.astype(BF16)
                    low = (v - high.astype(F32)).astype(BF16)
                    at = b * n + cl * GROUP
                    cut = slice(parity * width, (parity + 1) * width)
                    kept_ref[at : at + 16, cut] = high
                    kept_ref[full * n + at : full * n + at + 16, cut] = low
    packed = lax.dot_general(
        kept_ref[...], rep_ref[...], (((1,), (1,)), ((), ())), preferred_element_type=F32
    )
    packed = packed[: full * n] + packed[full * n :]
    for b in range(full):
        v = jnp.swapaxes(packed[b * n : (b + 1) * n].reshape(CL, GROUP, RBLOCK), 0, 1)
        for c in range(C):
            out_ref[:, c, :, b * RBLOCK : (b + 1) * RBLOCK] = v[:, c * L : (c + 1) * L]
    for r in range(full * RBLOCK, R):
        row = leg_ref[r].astype(F32)
        masks = tail_masks(low_ref, total, J)
        for cl in range(CL):
            rows = fold_ref[r % 2, cl * 16 : (cl + 1) * 16, :].astype(F32)
            v = jnp.where(masks[0], rows[:GROUP], jnp.where(masks[1], rows[GROUP:], 0.0))
            v = jnp.sum(v * row, axis=1, keepdims=True)
            out_ref[:, cl // L, cl % L, r : r + 1] = v


def whole(shape):
    return pl.BlockSpec(shape, lambda *_: (0,) * len(shape))


SMEM = pl.BlockSpec(memory_space=pltpu.SMEM)


def exchange(sent, count):
    if len(sent) == 1:
        return [lax.all_to_all(sent[0], "wave", 0, 0, tiled=True)]
    parts = [sent[0]]
    for d in range(1, count):
        parts.append(lax.ppermute(sent[d], "wave", [(i, i ^ d) for i in range(count)]))
    return parts


def travel_shapes(W, groups, width, apart=True):
    if XOR_ORDER(W) and apart:
        return [jax.ShapeDtypeStruct((groups, 32, width), BF16)] * W
    return [jax.ShapeDtypeStruct((W, groups, 32, width), BF16)]


def group_spec(shape, first):
    if len(shape) == 3:
        return pl.BlockSpec((1,) + shape[1:], lambda g: (g + first, 0, 0))
    return pl.BlockSpec((shape[0], 1) + shape[2:], lambda g: (0, g + first, 0, 0))


def shards(spectral, legendre, quad_weights, pair_order, lon_counts, vertical, wind_field):
    W, Z = lax.axis_size("wave"), lax.axis_size("lev")
    pairs, C, L, R = spectral.shape
    J = legendre.shape[2]
    band, NX = wind_field.shape[0], wind_field.shape[2]
    CL, LJ, total = C * L, L * band, R - 1
    me, z = lax.axis_index("wave"), lax.axis_index("lev")
    padded = -(-pairs // GROUP) * GROUP
    NG = padded // GROUP
    chunks = pieces(LEVEL_PIECES, NG)
    pads = padded - pairs

    own = spectral.transpose(1, 2, 0, 3).reshape(CL, pairs, R)
    own = jnp.pad(own, ((0, 0), (0, pads), (0, 0)))
    table = jnp.pad(legendre.transpose(1, 0, 2), ((0, 0), (0, pads), (0, 0)))

    own_pairs = pair_order.reshape(W, pairs)
    all_pairs = jnp.pad(own_pairs, ((0, 0), (0, pads)))
    lows = lax.dynamic_index_in_dim(all_pairs, me, 0, keepdims=False)
    lows = jnp.broadcast_to(lows[:, None], (padded, 128))
    if XOR_ORDER(W):
        all_pairs = all_pairs[me ^ jnp.arange(W)]
    all_pairs = all_pairs.reshape(W, NG, 1, GROUP)
    others = total - 1 - all_pairs
    is_odd = (all_pairs & 1) == 1
    evens = jnp.where(is_odd, others, all_pairs)
    waves = jnp.stack([evens, total - 1 - evens]).transpose(0, 2, 1, 3, 4)
    rows = NG * W * 16
    waves = jnp.broadcast_to(waves, (2, NG, W, 2, GROUP)).reshape(2, rows, 1)
    waves = jnp.broadcast_to(waves, (2, rows, 128))

    lane = np.arange(RBLOCK * GROUP)[None, :]
    half_width = RBLOCK * GROUP // 2
    rep = np.arange(RBLOCK)[:, None] == lane % half_width // GROUP * 2 + lane // half_width
    rep = jnp.asarray(rep, BF16)
    flip = jnp.asarray(np.arange(128)[:, None] + np.arange(128)[None, :] == 127, BF16)
    counts = lax.dynamic_slice_in_dim(lon_counts, me * band, band)
    counts = jnp.tile(counts, L)[None, :]
    wind = wind_field.transpose(1, 0, 2).reshape(LJ, NX)
    me_arr = me.astype(jnp.int32).reshape(1)
    quad = quad_weights[None, :]
    shapes = (CL, L, C, R, J, W, band)

    vert = vertical.astype(F32).reshape(Z, L, Z, L)

    def vblock(rows, cols):
        v = lax.dynamic_index_in_dim(vert, rows, 0, keepdims=False)
        return lax.dynamic_index_in_dim(v, cols, 1, keepdims=False)

    leg_spec = pl.BlockSpec(memory_space=pl.ANY)
    leg_scratch = [pltpu.VMEM((2, R, GROUP, J), BF16), pltpu.SemaphoreType.DMA((2, len(TABLE_CUTS) + 1))]
    low_spec = lambda g0: pl.BlockSpec((GROUP, 128), lambda g: (g + g0, 0))

    HX = NX // 2
    steps = 5 if rows % 640 == 0 else 1
    per = rows // steps
    bspec = pl.BlockSpec((per, HX), lambda i: (i, 0))
    bases = pl.pallas_call(
        functools.partial(basis_kernel, steps=HX // 128, NX=NX),
        grid=(steps,),
        out_shape=[jax.ShapeDtypeStruct((rows, HX), BF16)] * 2,
        in_specs=[pl.BlockSpec((2, per, 128), lambda i: (0, i, 0))],
        out_specs=[bspec, bspec],
        compiler_params=params(),
        cost_estimate=pl.CostEstimate(
            flops=rows * HX * 8, bytes_accessed=rows * HX * 4, transcendentals=0
        ),
        name="basis",
    )(waves)

    gathered, sums = [], []
    for g0, G in chunks:
        x = own[:, g0 * GROUP : (g0 + G) * GROUP][None]
        if Z == 4:
            if len(sums) >= AFTER:
                x, _ = lax.optimization_barrier((x, sums[-AFTER]))
            a = lax.ppermute(x, "lev", [(i, i ^ 1) for i in range(4)])
            if EARLY and g0 + G == NG:
                a, wind, counts = lax.optimization_barrier((a, wind, counts))
            table_d = jnp.stack([vblock(z ^ 2, z), vblock(z ^ 2, z ^ 1)])
            spec = pl.BlockSpec((1, CL, GROUP, R), lambda g: (0, 0, g, 0))
            part = pl.pallas_call(
                functools.partial(mix_kernel, L=L, C=C),
                grid=(G,),
                out_shape=jax.ShapeDtypeStruct(x.shape, BF16),
                in_specs=[SMEM, spec, spec],
                out_specs=spec,
                compiler_params=params(),
                name="partial_levels",
            )(table_d, x, a)
            sums.append(part)
            d = lax.ppermute(part, "lev", [(i, i ^ 2) for i in range(4)])
            gathered.append(((x, a), d, jnp.stack([vblock(z, z), vblock(z, z ^ 1)])))
        else:
            every = lax.all_gather(x, "lev", axis=0, tiled=True)
            tab = lax.dynamic_index_in_dim(vert, z, 0, keepdims=False).transpose(1, 0, 2)
            gathered.append(((every,), None, tab))

    parts, places = [], []
    for (g0, G), (srcs, extra, tab) in zip(chunks, gathered):
        specs = [
            pl.BlockSpec((s.shape[0], CL, GROUP, R), lambda g: (0, 0, g, 0)) for s in srcs
        ]
        args = list(srcs)
        if extra is not None:
            specs.append(pl.BlockSpec((1, CL, GROUP, R), lambda g: (0, 0, g, 0)))
            args.append(extra)
        fixed = [me_arr, tab, lows, rep, flip, table, *args]
        shaped = travel_shapes(W, G, LJ, not NATIVE or g0 + G == NG)
        sent = pl.pallas_call(
            functools.partial(
                inverse_kernel, shapes=shapes, n_src=len(srcs), extra=extra is not None, first=g0,
                n_out=len(shaped),
            ),
            grid=(G,),
            out_shape=shaped,
            in_specs=[SMEM, SMEM, low_spec(g0), whole(rep.shape), whole(flip.shape), leg_spec]
            + specs,
            out_specs=[group_spec(v.shape, 0) for v in shaped],
            scratch_shapes=[
                pltpu.VMEM((W, 32, LJ), BF16),
                pltpu.VMEM((CL, GROUP, R), F32),
                pltpu.VMEM((2, CL * 16, R // RBLOCK * RBLOCK * GROUP // 2), BF16),
            ]
            + leg_scratch,
            compiler_params=params(),
            cost_estimate=pl.CostEstimate(
                flops=2 * G * CL * 16 * R * GROUP * J,
                bytes_accessed=G * R * GROUP * J * 2,
                transcendentals=0,
            ),
            name="inverse_legendre",
        )(*fixed)
        for d, part in enumerate(exchange(sent, W)):
            parts.append(part)
            places.append((g0, d))

    XB = 256
    half = HX // XB
    chunks = tuple(pieces(BACK_PIECES, NG))
    apart = [not NATIVE_BACK or g0 == 0 for g0, _ in chunks]
    travel = [travel_shapes(W, G, LJ, one) for (_, G), one in zip(chunks, apart)]
    shaped = [v for piece in travel for v in piece]
    sent = pl.pallas_call(
        functools.partial(grid_kernel, places=tuple(places), W=W, chunks=chunks,
            counts_out=tuple(len(piece) for piece in travel), NX=NX,
        ),
        grid=(half,),
        out_shape=shaped,
        in_specs=[SMEM, whole(counts.shape)]
        + [whole(p.shape) for p in parts]
        + [pl.BlockSpec((rows, XB), lambda i: (0, i))] * 2
        + [
            whole(waves.shape),
            pl.BlockSpec((LJ, XB), lambda i: (0, i)),
            pl.BlockSpec((LJ, XB), lambda i: (0, i + half)),
        ],
        out_specs=[whole(v.shape) for v in shaped],
        scratch_shapes=[
            pltpu.VMEM((2, rows, LJ), BF16),
            pltpu.VMEM((2, LJ, rows), BF16),
            pltpu.VMEM((2, rows, LJ), F32),
        ],
        compiler_params=params(),
        cost_estimate=pl.CostEstimate(
            flops=4 * rows * LJ * NX, bytes_accessed=2 * NX * (rows + LJ), transcendentals=0
        ),
        name="grid_points",
    )(me_arr, counts, *parts, *bases, waves, wind, wind)

    out = None
    arrived, at = [], 0
    for piece in travel:
        arrived.append(exchange(sent[at : at + len(piece)], W))
        at += len(piece)
    for (g0, G), returned in zip(chunks, arrived):
        ospec = pl.BlockSpec((GROUP, C, L, R), lambda g, g0=g0: (g + g0, 0, 0, 0))
        before = [] if out is None else [out]
        fixed = [me_arr, lows, rep, flip, quad, table, *returned]
        out = pl.pallas_call(
            functools.partial(
                forward_kernel, shapes=shapes, n_parts=len(returned), first=g0
            ),
            grid=(G,),
            out_shape=jax.ShapeDtypeStruct((padded, C, L, R), F32),
            in_specs=[
                SMEM, low_spec(g0), whole(rep.shape), whole(flip.shape), whole(quad.shape),
                leg_spec,
            ]
            + [group_spec(p.shape, 0) for p in returned]
            + [pl.BlockSpec(memory_space=pl.ANY)] * len(before),
            out_specs=ospec,
            scratch_shapes=[
                pltpu.VMEM((W, 32, LJ), F32),
                pltpu.VMEM((2, CL * 16, J), BF16),
                pltpu.VMEM((2 * (R // RBLOCK) * CL * GROUP, RBLOCK * GROUP), BF16),
            ]
            + leg_scratch,
            input_output_aliases={len(fixed): 0} if before else {},
            compiler_params=params(),
            cost_estimate=pl.CostEstimate(
                flops=2 * G * CL * 16 * R * GROUP * J,
                bytes_accessed=G * R * GROUP * J * 2,
                transcendentals=0,
            ),
            name="forward_legendre",
        )(*fixed, *before)
    return out[:pairs]


def solution(mesh):
    return jax.shard_map(
        shards,
        mesh=mesh,
        in_specs=(
            P("wave", None, "lev", None),
            P("wave", None, None),
            P(),
            P(),
            P(),
            P(),
            P("wave", "lev", None),
        ),
        out_specs=P("wave", None, "lev", None),
        check_vma=False,
    )
```
